256 devices in a mesh: row: 16 (over x, y), col: 16 (over z, core).
Axes of the slice: x: 4, y: 4, z: 8, core: 2. Of those that a mesh axis runs over, the one named last changes fastest.
Arguments:
- trailing_slab: float32 [131072, 2048], P('row', 'col'), may hold values from -6 to 6, as said below
- panel_columns: float32 [32, 131072], P(None, 'row'), may hold values from -1870.1934 to 1870.1934
- far_image: float32 [32, 131072], P(None, 'row'), may hold values from -2048 to 2048
Outputs:
- updated_slab: float32 [131072, 2048], P('row', 'col')
- update_factor: float32 [32, 131072], P(None, 'row')
The draws below stay inside these ranges and needn't reach their ends.
Inputs may be any that keep to these rules, and one draw needn't show every extreme that they name: Rows 0 to 2047 of trailing_slab form a symmetric block.
All inputs are finite; a program needn't handle non-finite values.
Results may differ from the reference program's by a relative error of at most 0.0003.
Values sent between devices are 32-bit elements; how exact they have to be, the bound alone decides.
A program may use at most 64 MiB of HBM per device.

```python
import math
import jax
import jax.numpy as jnp
from jax import lax

NB = 32
ORDER = 131072
SLAB = 2048


def draw_trailing_slab(key, part):
    first = jax.random.fold_in(key, 0)
    values = jax.random.truncated_normal(first, -6.0, 6.0, (ORDER, SLAB), jnp.float32)
    block = values[:SLAB]
    mirrored = 0.5 * (block + block.T)
    return jnp.concatenate([mirrored, values[SLAB:]], axis=0)


def draw_panel_columns(key, part):
    first = jax.random.fold_in(key, 0)
    second = jax.random.fold_in(key, 1)
    fourth = jax.random.fold_in(key, 3)
    values = jax.random.truncated_normal(first, -6.0, 6.0, (NB, ORDER), jnp.float32)
    magnitude = 1.0 + 2.0 * jax.random.uniform(second, (NB,), jnp.float32)
    signs = (2 * jax.random.randint(fourth, (NB,), 0, 2) - 1).astype(jnp.float32)
    diagonal = jnp.diag(signs * magnitude * jnp.float32(math.sqrt(ORDER)))
    head_rows = values[:, :NB] + diagonal
    return jnp.concatenate([head_rows, values[:, NB:]], axis=1)


def steps_of(rng, extent, cuts, least, top_value):
    level = 1.0
    for dim, parts in cuts:
        steps = jax.random.uniform(jax.random.fold_in(jax.random.fold_in(rng, 6), dim), (parts,), jnp.float32, least / len(cuts), top_value / len(cuts))
        level = level * jnp.repeat(jnp.exp(steps), extent[dim] // parts).reshape((-1,) + (1,) * (len(extent) - 1 - dim))
    return level


def gaussian(key, shape, deviation, limit, cuts=(), held_as=jnp.bfloat16):
    factor_of = steps_of(key, shape, cuts, -0.22, 0.18) if cuts else 1.0
    array = jax.random.normal(key, shape, jnp.float32) * deviation * factor_of
    return jnp.minimum(jnp.maximum(array, -limit), limit).astype(held_as)


def setup_inputs(seed: int = 0) -> dict:
    splits = jax.random.split(jax.random.key(seed), 4)
    trailing_slab = draw_trailing_slab(jax.random.fold_in(splits[3], 71), 0)
    panel_columns = draw_panel_columns(jax.random.fold_in(splits[3], 71), 0)
    far_image = gaussian(splits[2], (NB, ORDER), (ORDER ** 0.5), 2048.0, ((1, 16),), jnp.float32)
    return {"trailing_slab": trailing_slab, "panel_columns": panel_columns, "far_image": far_image}


def product(left, right):
    return jnp.dot(left, right, precision=lax.Precision.HIGHEST, preferred_element_type=jnp.float32)

def contract(left, right, left_dim, right_dim):
    return lax.dot_general(left, right, (((left_dim,), (right_dim,)), ((), ())), precision=lax.Precision.HIGHEST, preferred_element_type=jnp.float32)

def cholesky_rows(gram_total):
    panel_width = gram_total.shape[0]
    identity = jnp.eye(panel_width, dtype=jnp.float32)
    indices = jnp.arange(panel_width)
    lower_part = jnp.zeros((panel_width, panel_width), jnp.float32)
    for column in range(panel_width):
        onehot = identity[column]
        residue = gram_total[:, column] - product(lower_part, lower_part[column])
        pivot = jnp.sqrt(jnp.sum(residue * onehot))
        new_column = jnp.where(indices >= column, residue / pivot, 0.0)
        lower_part = lower_part + new_column[:, None] * onehot[None, :]
    return lower_part

def invert_lower(lower_part):
    panel_width = lower_part.shape[0]
    identity = jnp.eye(panel_width, dtype=jnp.float32)
    inverse = jnp.zeros((panel_width, panel_width), jnp.float32)
    for index_row in range(panel_width):
        onehot = identity[index_row]
        pivot = jnp.sum(lower_part[index_row] * onehot)
        new_row = (onehot - product(lower_part[index_row], inverse)) / pivot
        inverse = inverse + onehot[:, None] * new_row[None, :]
    return inverse

def decompose(shifted):
    panel_width = shifted.shape[0]
    identity = jnp.eye(panel_width, dtype=jnp.float32)
    indices = jnp.arange(panel_width)
    lower_unit = identity
    upper_part = shifted
    for column in range(panel_width):
        factor = jnp.where(indices > column, upper_part[:, column] / upper_part[column, column], 0.0)
        lower_unit = lower_unit + factor[:, None] * identity[column][None, :]
        upper_part = upper_part - factor[:, None] * upper_part[column][None, :]
    return (lower_unit, jnp.triu(upper_part))

def factors(gram_total, top_rows):
    panel_width = gram_total.shape[0]
    identity = jnp.eye(panel_width, dtype=jnp.float32)
    cholesky_lower = cholesky_rows(gram_total)
    cholesky_inverse = invert_lower(cholesky_lower)
    top_factor = product(cholesky_inverse, top_rows).T
    sign_flip = jnp.where(jnp.diag(top_factor) >= 0.0, -1.0, 1.0).astype(jnp.float32)
    lower_unit, upper_part = decompose(identity - top_factor * sign_flip[None, :])
    upper_inverse = invert_lower(upper_part.T).T
    root_inverse = cholesky_inverse.T
    mixing = -product(root_inverse * sign_flip[None, :], upper_inverse)
    lower_inverse = invert_lower(lower_unit)
    triangle = product(upper_part, lower_inverse.T)
    return (mixing, upper_inverse, triangle)

def reference(trailing_slab, panel_columns, far_image):
    gram_total = product(panel_columns, panel_columns.T)
    mixing, upper_inverse, triangle = factors(gram_total, panel_columns[:, :NB])
    reflectors = product(mixing.T, panel_columns)
    reflectors = reflectors.at[:, :NB].add(upper_inverse.T)
    slab_part = reflectors[:, :SLAB]
    images = contract(slab_part, trailing_slab, 1, 1) + product(mixing.T, far_image)
    inner_block = product(reflectors, images.T)
    core_block = product(product(triangle.T, inner_block), triangle)
    weights = product(triangle.T, images) - 0.5 * product(core_block.T, reflectors)
    slab_weights = weights[:, :SLAB]
    updated = trailing_slab - contract(reflectors, slab_weights, 0, 0) - contract(weights, slab_part, 0, 0)
    return (updated, weights)
```

```python
import functools

import jax
import jax.numpy as jnp
from jax import lax
from jax.experimental import pallas as pl
from jax.experimental.pallas import tpu as pltpu
from jax.sharding import PartitionSpec as P

F32 = jnp.float32
BF16 = jnp.bfloat16
MESH = pl.DeviceIdType.MESH
NT = (((1,), (1,)), ((), ()))
TN = (((0,), (0,)), ((), ()))
NN = (((1,), (0,)), ((), ()))


def exact(left, right, dims=NN):
    return lax.dot_general(
        left, right, dims, precision=lax.Precision.HIGHEST, preferred_element_type=F32
    )


def narrow(left, right, dims):
    return lax.dot_general(left, right, dims, preferred_element_type=F32)


def split(x):
    high = x.astype(BF16)
    low = (x - high.astype(F32)).astype(BF16)
    return high, low


def split3(x):
    high = x.astype(BF16)
    rest = x - high.astype(F32)
    mid = rest.astype(BF16)
    low = (rest - mid.astype(F32)).astype(BF16)
    return high, mid, low


def gram_of(block):
    nb = block.shape[0]
    one, two, three = split3(block)
    first = narrow(jnp.concatenate([one, two, three], 0), one, NT)
    second = narrow(jnp.concatenate([one, two], 0), two, NT)
    third = narrow(one, three, NT)
    return (
        first[:nb]
        + (first[nb : 2 * nb] + second[:nb])
        + (first[2 * nb :] + second[nb:] + third)
    )


def cross(left, right):
    nb = left.shape[0]
    lh, ll = split(left)
    rh, rl = split(right)
    both = narrow(jnp.concatenate([lh, ll], 0), rh, NT)
    return both[:nb] + both[nb:] + narrow(lh, rl, NT)


def eliminate(tables, nb):
    rows = lax.broadcasted_iota(jnp.int32, (nb, 128), 0)
    for j in range(nb):
        done = []
        for table in tables:
            column = jnp.broadcast_to(table[:, j : j + 1], (nb, 128))
            pivot_row = table[j : j + 1, :] / column[j : j + 1, :]
            done.append(table - jnp.where(rows > j, column, 0.0) * pivot_row)
        tables = done
    return tables


def pack(square):
    total = square[0:8]
    for k in range(1, 4):
        total = total + pltpu.roll(square[8 * k : 8 * k + 8], 32 * k, 1)
    return total


def unpack(packed, lanes):
    parts = [packed] + [pltpu.roll(packed, 128 - 32 * k, 1) for k in range(1, 4)]
    return jnp.where(lanes < 32, jnp.concatenate(parts, 0), 0.0)


def wide(square):
    return jnp.concatenate([square, jnp.zeros((square.shape[0], 128 - square.shape[1]), F32)], 1)


def exchange_kernel(
    nrow, ncol,
    slab, panel, far,
    images, coefs,
    pv, sv, fv, gsend, gbuf, headbuf, topbuf, pt, zout, pbuf, zsum, rbuf, zown,
    osend, obuf, h1send, h1buf, h2send, h2buf,
    load_sem, g_ssem, g_rsem, t_ssem, t_rsem, p_ssem, p_rsem, r_ssem, r_rsem,
    a_ssem, a_rsem, f_ssem, o_ssem, o_rsem, h1_ssem, h1_rsem, h2_ssem, h2_rsem,
    image_sem,
):
    nb = 32
    nz = ncol // 2
    chunk = pv.shape[1] // ncol
    row = lax.axis_index("row")
    col = lax.axis_index("col")
    z = lax.div(col, 2)
    core = lax.rem(col, 2)
    partner = col + 1 - 2 * core
    rows = lax.broadcasted_iota(jnp.int32, (nb, 128), 0)
    lanes = lax.broadcasted_iota(jnp.int32, (nb, 128), 1)

    def remote(src, dst, ssem, rsem, device):
        return pltpu.make_async_remote_copy(
            src_ref=src, dst_ref=dst, send_sem=ssem, recv_sem=rsem,
            device_id=device, device_id_type=MESH,
        )

    def row_peer(k):
        return lax.rem(row + k, nrow)

    def col_peer(k):
        return lax.rem(col + k, ncol)

    def z_peer(k):
        return lax.rem(z + k, nz)

    load_p = pltpu.make_async_copy(panel, pv, load_sem.at[0])
    load_s = pltpu.make_async_copy(slab, sv, load_sem.at[1])
    own = core * nz + z
    own_columns = pl.ds(pl.multiple_of(own * chunk, chunk), chunk)
    load_f = pltpu.make_async_copy(far.at[:, own_columns], fv, load_sem.at[2])
    load_p.start()
    load_s.start()
    load_f.start()

    barrier = pltpu.get_barrier_semaphore()

    @pl.loop(1, nrow)
    def _(k):
        pl.semaphore_signal(barrier, inc=1, device_id={"row": row_peer(k)}, device_id_type=MESH)

    @pl.loop(1, ncol)
    def _(k):
        pl.semaphore_signal(barrier, inc=1, device_id={"col": col_peer(k)}, device_id_type=MESH)

    load_p.wait()
    gram = jnp.zeros((nb, nb), F32)
    for g in range(ncol):
        gram = gram + gram_of(pv[:, g * chunk : (g + 1) * chunk])
    gsend[...] = pack(wide(gram))
    gbuf[row] = gsend[...]
    pl.semaphore_wait(barrier, nrow + ncol - 2)

    head_columns = pl.ds(pl.multiple_of(col * 128, 128), 128)

    @pl.when(row == 0)
    def _():
        local_head = pltpu.make_async_copy(pv.at[:, head_columns], headbuf, load_sem.at[3])
        local_top = pltpu.make_async_copy(pv.at[:, pl.ds(0, 128)], topbuf, load_sem.at[4])
        local_head.start()
        local_top.start()

        @pl.loop(1, nrow)
        def _(k):
            peer = row_peer(k)
            remote(topbuf_src(pv), topbuf, t_ssem.at[0, k], t_rsem.at[0], {"row": peer}).start()
            remote(pv.at[:, head_columns], headbuf, t_ssem.at[1, k], t_rsem.at[1], {"row": peer}).start()

        local_head.wait()
        local_top.wait()

    @pl.loop(1, nrow)
    def _(k):
        remote(gsend, gbuf.at[row], g_ssem.at[k], g_rsem.at[row], {"row": row_peer(k)}).start()

    @pl.when(row != 0)
    def _():
        remote(topbuf_src(pv), topbuf, t_ssem.at[0, 0], t_rsem.at[0], {"row": 0}).wait_recv()
        remote(pv.at[:, head_columns], headbuf, t_ssem.at[1, 0], t_rsem.at[1], {"row": 0}).wait_recv()

    @pl.loop(1, nrow)
    def _(k):
        peer = row_peer(k)
        remote(gsend, gbuf.at[peer], g_ssem.at[k], g_rsem.at[peer], {"row": peer}).wait_recv()

    total = gbuf[0]
    for r in range(1, nrow):
        total = total + gbuf[r]
    table = (
        unpack(total, lanes)
        + jnp.where(lanes == rows + nb, 1.0, 0.0)
        + pltpu.roll(jnp.where(lanes < nb, topbuf[...], 0.0), 2 * nb, 1)
    )
    (table,) = eliminate([table], nb)
    pivots = jnp.sum(jnp.where(lanes == rows, table, 0.0), axis=1, keepdims=True)
    table = table / jnp.sqrt(pivots)
    signs = jnp.sum(jnp.where(lanes == rows + 2 * nb, table, 0.0), axis=1, keepdims=True)
    flip = jnp.where(signs >= 0.0, -1.0, 1.0).astype(F32)
    upper = jnp.where((lanes >= rows) & (lanes < nb), table * flip, 0.0)
    unit = jnp.where(lanes == rows, 1.0, 0.0)[:, :nb]
    correction = wide(exact(upper[:, :nb], unit, TN))
    flipped_inverse = (pltpu.roll(table, 128 - nb, 1) * flip)[:, :nb]
    shifted_t = jnp.where(lanes == rows, 1.0, 0.0) - jnp.where(
        lanes < nb, pltpu.roll(table, 128 - 2 * nb, 1) * flip, 0.0
    )

    @pl.when(col == 0)
    def _():
        headbuf[...] = headbuf[...] - correction

    pt[...] = pv[...]

    @pl.when(row == 0)
    def _():
        pt[:, 0:128] = pt[:, 0:128] - correction

    load_s.wait()
    high, low = split(headbuf[...])
    weights = jnp.concatenate(
        [
            jnp.concatenate([high, high], 1),
            jnp.concatenate([low, jnp.zeros_like(low)], 1),
        ],
        0,
    )

    def image_chunk(index):
        block = sv[pl.ds(pl.multiple_of(index * chunk, chunk), chunk), :]
        sh, sl = split(block)
        both = narrow(weights, jnp.concatenate([sh, sl], 1), NT)
        return both[:nb] + both[nb:]

    @pl.loop(1, nz + 1)
    def _(k):
        peer = z_peer(k)
        zout[peer] = image_chunk((1 - core) * nz + peer)

    @pl.loop(1, nz + 1)
    def _(k):
        peer = z_peer(k)
        remote(zout.at[peer], pbuf.at[peer], p_ssem.at[peer], p_rsem.at[peer], {"col": partner}).start()

    @pl.loop(1, nz + 1)
    def _(k):
        peer = z_peer(k)
        part = image_chunk(core * nz + peer)
        remote(zout.at[peer], pbuf.at[peer], p_ssem.at[peer], p_rsem.at[peer], {"col": partner}).wait_recv()
        zsum[peer] = part + pbuf[peer]

    @pl.loop(1, nz)
    def _(k):
        peer = z_peer(k)
        remote(zsum.at[peer], rbuf.at[z], r_ssem.at[peer], r_rsem.at[z], {"col": 2 * peer + core}).start()

    load_f.wait()

    @pl.when(row == 0)
    def _():
        head = sv.shape[1] * ncol
        ph, plow = split(pt[:, 0:head])
        sh, sl = split(sv[0:head, :])
        both = narrow(jnp.concatenate([ph, plow], 0), sh, NN)
        osend[...] = both[:nb] + both[nb:] + narrow(ph, sl, NN)

    @pl.when(row == 0)
    def _():
        extra = pltpu.make_async_copy(far.at[:, head_columns], obuf, load_sem.at[5])
        extra.start()
        extra.wait()
        osend[...] = osend[...] + obuf[...]
        obuf[...] = osend[...]

        @pl.loop(1, nrow)
        def _(k):
            remote(osend, obuf, o_ssem.at[k], o_rsem, {"row": row_peer(k)}).start()

    inner = cross(fv[...], pt[:, own_columns])
    for g in range(nz):
        columns = pl.ds(pl.multiple_of((core * nz + g) * chunk, chunk), chunk)
        inner = inner + cross(zsum[g], pt[:, columns])
    h1send[...] = pack(wide(inner))
    h1buf[row] = h1send[...]

    @pl.loop(1, nrow)
    def _(k):
        remote(h1send, h1buf.at[row], h1_ssem.at[k], h1_rsem.at[row], {"row": row_peer(k)}).start()

    shifted = wide(exact(shifted_t[:, :nb], unit, TN))
    augment = jnp.where(lanes == rows + nb, 1.0, 0.0)
    lower_table, upper_table = eliminate([shifted + augment, shifted_t + augment], nb)
    diagonal = jnp.sum(jnp.where(lanes == rows, upper_table, 0.0), axis=1, keepdims=True)
    lower_inverse = pltpu.roll(lower_table, 128 - nb, 1)[:, :nb]
    upper_inverse_t = (pltpu.roll(upper_table, 128 - nb, 1) / diagonal)[:, :nb]
    mixing_t = -exact(upper_inverse_t, flipped_inverse)
    second_t = -exact(lower_inverse, flipped_inverse)
    kernel_t = exact(second_t, mixing_t, TN)
    own_reflectors = exact(mixing_t, headbuf[...])
    bottom = exact(second_t, own_reflectors, TN)

    @pl.loop(1, nrow)
    def _(k):
        peer = row_peer(k)
        remote(h1send, h1buf.at[peer], h1_ssem.at[k], h1_rsem.at[peer], {"row": peer}).wait_recv()

    share = h1buf[0]
    for r in range(1, nrow):
        share = share + h1buf[r]
    h2send[...] = share
    h2buf[col] = share

    @pl.loop(1, nz)
    def _(k):
        peer = z_peer(k)
        remote(zsum.at[peer], rbuf.at[peer], r_ssem.at[peer], r_rsem.at[peer], {"col": 2 * peer + core}).wait_recv()

    rbuf[z] = zsum[z]
    chunk_sum = fv[...]
    for r in range(nz):
        chunk_sum = chunk_sum + rbuf[r]
    zown[...] = chunk_sum

    @pl.loop(1, ncol)
    def _(k):
        remote(h2send, h2buf.at[col], h2_ssem.at[k], h2_rsem.at[col], {"col": col_peer(k)}).start()

    keep = pltpu.make_async_copy(zown, images.at[own], image_sem)
    keep.start()
    remote(zown, images.at[own], f_ssem.at[z], a_rsem.at[own], {"col": partner}).start()

    @pl.loop(1, nz)
    def _(k):
        peer = z_peer(k)
        remote(zown, images.at[own], a_ssem.at[peer], a_rsem.at[own], {"col": 2 * peer + core}).start()

    @pl.when(row != 0)
    def _():
        remote(osend, obuf, o_ssem.at[0], o_rsem, {"row": 0}).wait_recv()

    @pl.loop(1, ncol)
    def _(k):
        peer = col_peer(k)
        remote(h2send, h2buf.at[peer], h2_ssem.at[k], h2_rsem.at[peer], {"col": peer}).wait_recv()

    inner_total = h2buf[0]
    for c in range(1, ncol):
        inner_total = inner_total + h2buf[c]
    inner_t = unpack(inner_total, lanes)[:, :nb]
    weight_t = -0.5 * exact(exact(second_t, inner_t), kernel_t)
    own_weights = exact(second_t, obuf[...]) + exact(weight_t, headbuf[...])
    top_part = exact(mixing_t, own_weights, TN) + exact(weight_t, own_reflectors, TN)
    coefs[0:nb, :] = top_part
    coefs[nb : 2 * nb, :] = bottom
    coefs[2 * nb : 3 * nb, :] = wide(jnp.concatenate([weight_t, second_t], 1))
    coefs[3 * nb :, :] = jnp.where(row == 0, correction, 0.0)

    def gathered(index, ssem):
        slot = images.at[index]
        return remote(slot, slot, ssem, a_rsem.at[index], {"col": partner})

    @pl.loop(1, nz)
    def _(k):
        peer = z_peer(k)
        copy = gathered(core * nz + peer, f_ssem.at[peer])
        copy.wait_recv()
        copy.start()

    @pl.loop(0, nz)
    def _(k):
        peer = z_peer(k)
        gathered((1 - core) * nz + peer, f_ssem.at[peer]).wait_recv()

    keep.wait()

    @pl.loop(0, nz)
    def _(k):
        remote(zout.at[k], pbuf.at[k], p_ssem.at[k], p_rsem.at[k], {"col": partner}).wait_send()
        gathered(core * nz + k, f_ssem.at[k]).wait_send()

    @pl.loop(1, nz)
    def _(k):
        peer = z_peer(k)
        device = {"col": 2 * peer + core}
        remote(zsum.at[peer], rbuf.at[z], r_ssem.at[peer], r_rsem.at[z], device).wait_send()
        remote(zown, images.at[own], a_ssem.at[peer], a_rsem.at[own], device).wait_send()

    @pl.loop(1, nrow)
    def _(k):
        device = {"row": row_peer(k)}
        remote(gsend, gbuf.at[row], g_ssem.at[k], g_rsem.at[row], device).wait_send()
        remote(h1send, h1buf.at[row], h1_ssem.at[k], h1_rsem.at[row], device).wait_send()

    @pl.loop(1, ncol)
    def _(k):
        remote(h2send, h2buf.at[col], h2_ssem.at[k], h2_rsem.at[col], {"col": col_peer(k)}).wait_send()

    @pl.when(row == 0)
    def _():
        @pl.loop(1, nrow)
        def _(k):
            device = {"row": row_peer(k)}
            remote(topbuf_src(pv), topbuf, t_ssem.at[0, k], t_rsem.at[0], device).wait_send()
            remote(pv.at[:, head_columns], headbuf, t_ssem.at[1, k], t_rsem.at[1], device).wait_send()
            remote(osend, obuf, o_ssem.at[k], o_rsem, device).wait_send()


def topbuf_src(pv):
    return pv.at[:, pl.ds(0, 128)]


def update_kernel(slab, panel, images, coefs, updated, factor, xs):
    nb = 32
    parts = images.shape[0]
    chunk = images.shape[2]
    first = pl.program_id(0) == 0
    bh, bl = split(coefs[0 : 2 * nb, :])
    right = jnp.concatenate([bh, bl, bh], 0)
    ch, cl = split(coefs[2 * nb : 3 * nb, 0 : 2 * nb])
    left = jnp.concatenate([ch, ch, cl], 1)
    xs[:nb, :] = panel[...]

    @pl.when(first)
    def _():
        xs[:nb, 0:128] = xs[:nb, 0:128] - coefs[3 * nb :, :]

    for g in range(parts):
        xs[nb:, g * chunk : (g + 1) * chunk] = images[g]
    for g in range(parts):
        piece = slice(g * chunk, (g + 1) * chunk)
        xh, xl = split(xs[:, piece])
        factor[:, piece] = narrow(left, jnp.concatenate([xh, xl, xh], 0), NN)
        stacked = jnp.concatenate([xh, xh, xl], 0)
        updated[piece, :] = slab[piece, :] - narrow(stacked, right, TN)


def local(nrow, ncol, slab, panel, far):
    nb, length = panel.shape
    chunk = length // ncol
    nz = ncol // 2
    anywhere = pl.BlockSpec(memory_space=pl.ANY)
    vmem = pl.BlockSpec(memory_space=pltpu.VMEM)
    dma = pltpu.SemaphoreType.DMA
    images, coefs = pl.pallas_call(
        functools.partial(exchange_kernel, nrow, ncol),
        name="exchange",
        out_shape=(
            jax.ShapeDtypeStruct((ncol, nb, chunk), F32),
            jax.ShapeDtypeStruct((4 * nb, 128), F32),
        ),
        in_specs=[anywhere] * 3,
        out_specs=(anywhere, vmem),
        scratch_shapes=[
            pltpu.VMEM((nb, length), F32),
            pltpu.VMEM(slab.shape, F32),
            pltpu.VMEM((nb, chunk), F32),
            pltpu.VMEM((8, 128), F32),
            pltpu.VMEM((nrow, 8, 128), F32),
            pltpu.VMEM((nb, 128), F32),
            pltpu.VMEM((nb, 128), F32),
            pltpu.VMEM((nb, length), F32),
            pltpu.VMEM((nz, nb, chunk), F32),
            pltpu.VMEM((nz, nb, chunk), F32),
            pltpu.VMEM((nz, nb, chunk), F32),
            pltpu.VMEM((nz, nb, chunk), F32),
            pltpu.VMEM((nb, chunk), F32),
            pltpu.VMEM((nb, 128), F32),
            pltpu.VMEM((nb, 128), F32),
            pltpu.VMEM((8, 128), F32),
            pltpu.VMEM((nrow, 8, 128), F32),
            pltpu.VMEM((8, 128), F32),
            pltpu.VMEM((ncol, 8, 128), F32),
            dma((6,)),
            dma((nrow,)), dma((nrow,)),
            dma((2, nrow)), dma((2,)),
            dma((nz,)), dma((nz,)),
            dma((nz,)), dma((nz,)),
            dma((nz,)), dma((ncol,)), dma((nz,)),
            dma((nrow,)), dma(()),
            dma((nrow,)), dma((nrow,)),
            dma((ncol,)), dma((ncol,)),
            dma(()),
        ],
        compiler_params=pltpu.CompilerParams(
            collective_id=0, has_side_effects=True, vmem_limit_bytes=32 * 2**20
        ),
    )(slab, panel, far)
    steps = 4
    wide_rows = length // steps
    parts = ncol // steps
    return pl.pallas_call(
        update_kernel,
        name="update",
        grid=(steps,),
        out_shape=(
            jax.ShapeDtypeStruct(slab.shape, F32),
            jax.ShapeDtypeStruct(panel.shape, F32),
        ),
        in_specs=[
            pl.BlockSpec((wide_rows, 128), lambda i: (i, 0)),
            pl.BlockSpec((nb, wide_rows), lambda i: (0, i)),
            pl.BlockSpec((parts, nb, chunk), lambda i: (i, 0, 0)),
            pl.BlockSpec((4 * nb, 128), lambda i: (0, 0)),
        ],
        out_specs=(
            pl.BlockSpec((wide_rows, 128), lambda i: (i, 0)),
            pl.BlockSpec((nb, wide_rows), lambda i: (0, i)),
        ),
        scratch_shapes=[pltpu.VMEM((2 * nb, wide_rows), F32)],
        compiler_params=pltpu.CompilerParams(vmem_limit_bytes=32 * 2**20),
    )(slab, panel, images, coefs)


def solution(mesh):
    sizes = dict(mesh.shape)
    body = functools.partial(local, sizes["row"], sizes["col"])
    in_specs = (P("row", "col"), P(None, "row"), P(None, "row"))
    out_specs = (P("row", "col"), P(None, "row"))
    return jax.shard_map(body, mesh=mesh, in_specs=in_specs, out_specs=out_specs, check_vma=False)
```

```python
import functools

import jax
import jax.numpy as jnp
from jax import lax
from jax.experimental import pallas as pl
from jax.experimental.pallas import tpu as pltpu
from jax.sharding import PartitionSpec as P

F32 = jnp.float32
BF16 = jnp.bfloat16
MESH = pl.DeviceIdType.MESH
NT = (((1,), (1,)), ((), ()))
TN = (((0,), (0,)), ((), ()))
NN = (((1,), (0,)), ((), ()))


def exact(left, right, dims=NN):
    return lax.dot_general(
        left, right, dims, precision=lax.Precision.HIGHEST, preferred_element_type=F32
    )


def narrow(left, right, dims):
    return lax.dot_general(left, right, dims, preferred_element_type=F32)


def split(x):
    high = x.astype(BF16)
    low = (x - high.astype(F32)).astype(BF16)
    return high, low


def split3(x):
    high = x.astype(BF16)
    rest = x - high.astype(F32)
    mid = rest.astype(BF16)
    low = (rest - mid.astype(F32)).astype(BF16)
    return high, mid, low


def gram_of(block):
    nb = block.shape[0]
    one, two, three = split3(block)
    first = narrow(jnp.concatenate([one, two, three], 0), one, NT)
    second = narrow(jnp.concatenate([one, two], 0), two, NT)
    third = narrow(one, three, NT)
    return (
        first[:nb]
        + (first[nb : 2 * nb] + second[:nb])
        + (first[2 * nb :] + second[nb:] + third)
    )


def cross(left, right):
    nb = left.shape[0]
    lh, ll = split(left)
    rh, rl = split(right)
    both = narrow(jnp.concatenate([lh, ll], 0), rh, NT)
    return both[:nb] + both[nb:] + narrow(lh, rl, NT)


def eliminate(tables, nb):
    rows = lax.broadcasted_iota(jnp.int32, (nb, 128), 0)
    for j in range(nb):
        done = []
        for table in tables:
            column = jnp.broadcast_to(table[:, j : j + 1], (nb, 128))
            pivot_row = table[j : j + 1, :] / column[j : j + 1, :]
            done.append(table - jnp.where(rows > j, column, 0.0) * pivot_row)
        tables = done
    return tables


def pack(square):
    total = square[0:8]
    for k in range(1, 4):
        total = total + pltpu.roll(square[8 * k : 8 * k + 8], 32 * k, 1)
    return total


def unpack(packed, lanes):
    parts = [packed] + [pltpu.roll(packed, 128 - 32 * k, 1) for k in range(1, 4)]
    return jnp.where(lanes < 32, jnp.concatenate(parts, 0), 0.0)


def wide(square):
    return jnp.concatenate([square, jnp.zeros((square.shape[0], 128 - square.shape[1]), F32)], 1)


def exchange_kernel(
    nrow, ncol,
    slab, panel, far,
    images, coefs,
    pv, sv, fv, gsend, gbuf, headbuf, pt, zout, pbuf, zsum,
    leaf3, leaf4, near, relay, twos, zown, osend, obuf, h1send, h1buf, h2send, h2buf,
    load_sem, g_ssem, g_rsem, t_ssem, t_rsem, p_ssem, p_rsem, r_ssem, r_rsem,
    a_ssem, a_rsem, f_ssem, f_rsem, o_ssem, o_rsem, h1_ssem, h1_rsem, h2_ssem, h2_rsem,
    image_sem,
):
    nb = 32
    nz = ncol // 2
    chunk = pv.shape[1] // ncol
    half = chunk // 2
    row = lax.axis_index("row")
    col = lax.axis_index("col")
    z = lax.div(col, 2)
    core = lax.rem(col, 2)
    partner = {"col": col + 1 - 2 * core}
    rows = lax.broadcasted_iota(jnp.int32, (nb, 128), 0)
    lanes = lax.broadcasted_iota(jnp.int32, (nb, 128), 1)

    def remote(src, dst, ssem, rsem, device):
        return pltpu.make_async_remote_copy(
            src_ref=src, dst_ref=dst, send_sem=ssem, recv_sem=rsem,
            device_id=device, device_id_type=MESH,
        )

    def row_peer(k):
        return lax.rem(row + k, nrow)

    def col_peer(k):
        return lax.rem(col + k, ncol)

    def z_peer(k):
        return lax.rem(z + k + nz, nz)

    def chip(k):
        return {"col": 2 * z_peer(k) + core}

    load_p = pltpu.make_async_copy(panel, pv, load_sem.at[0])
    load_s = pltpu.make_async_copy(slab, sv, load_sem.at[1])
    own = core * nz + z
    own_columns = pl.ds(pl.multiple_of(own * chunk, chunk), chunk)
    load_f = pltpu.make_async_copy(far.at[:, own_columns], fv, load_sem.at[2])
    load_p.start()
    load_s.start()
    load_f.start()

    barrier = pltpu.get_barrier_semaphore()

    @pl.loop(1, nrow)
    def _(k):
        pl.semaphore_signal(barrier, inc=1, device_id={"row": row_peer(k)}, device_id_type=MESH)

    for device in (partner, chip(1), chip(-1), chip(2), chip(-2)):
        pl.semaphore_signal(barrier, inc=1, device_id=device, device_id_type=MESH)

    load_p.wait()
    gram = jnp.zeros((nb, nb), F32)
    for g in range(ncol):
        gram = gram + gram_of(pv[:, g * chunk : (g + 1) * chunk])
    gsend[0:8, :] = pack(wide(gram))
    gsend[8:16, :] = pack(jnp.where(lanes < nb, pv[:, 0:128], 0.0))
    gbuf[row] = gsend[...]
    pt[...] = pv[...]
    pl.semaphore_wait(barrier, nrow + 4)

    head_columns = pl.ds(pl.multiple_of(col * 128, 128), 128)

    @pl.when(row == 0)
    def _():
        @pl.loop(1, nrow)
        def _(k):
            remote(pv.at[:, head_columns], headbuf, t_ssem.at[k], t_rsem, {"row": row_peer(k)}).start()

    @pl.loop(1, nrow)
    def _(k):
        remote(gsend, gbuf.at[row], g_ssem.at[k], g_rsem.at[row], {"row": row_peer(k)}).start()

    @pl.when(row == 0)
    def _():
        local_head = pltpu.make_async_copy(pv.at[:, head_columns], headbuf, load_sem.at[3])
        local_head.start()
        local_head.wait()

    load_s.wait()

    @pl.when(row != 0)
    def _():
        remote(pv.at[:, head_columns], headbuf, t_ssem.at[0], t_rsem, {"row": 0}).wait_recv()

    def produce():
        high, low = split(headbuf[...])
        weights = jnp.concatenate(
            [
                jnp.concatenate([high, high], 1),
                jnp.concatenate([low, jnp.zeros_like(low)], 1),
            ],
            0,
        )

        def product(index):
            block = sv[pl.ds(pl.multiple_of(index * chunk, chunk), chunk), :]
            sh, sl = split(block)
            both = narrow(weights, jnp.concatenate([sh, sl], 1), NT)
            return both[:nb] + both[nb:]

        def to_partner(peer):
            return remote(zout.at[peer], pbuf.at[peer], p_ssem.at[peer], p_rsem.at[peer], partner)

        def other_half(k):
            peer = z_peer(k)
            zout[peer] = product((1 - core) * nz + peer)

            @pl.when(k > 3)
            def _():
                to_partner(z_peer(k - 1)).start()

        def own_half(k):
            peer = z_peer(k)
            part = product(core * nz + peer)
            to_partner(peer).wait_recv()
            zsum[peer] = part + pbuf[peer]

        pl.loop(3, nz + 3)(other_half)
        to_partner(z_peer(nz + 2)).start()
        pl.loop(3, nz - 2)(own_half)
        pl.loop(nz - 2, nz + 3)(own_half)
        stage_one(lambda copy: copy.start())

    def stage_one(act):
        act(remote(zsum.at[z_peer(-3)], leaf3.at[0], r_ssem.at[0], r_rsem.at[0], chip(-1)))
        act(remote(zsum.at[z_peer(3)], leaf3.at[1], r_ssem.at[1], r_rsem.at[1], chip(1)))
        first = zsum.at[z_peer(4), :, pl.ds(0, half)]
        second = zsum.at[z_peer(4), :, pl.ds(half, half)]
        act(remote(first, leaf4.at[0], r_ssem.at[2], r_rsem.at[2], chip(-2)))
        act(remote(second, leaf4.at[1], r_ssem.at[3], r_rsem.at[3], chip(2)))
        act(remote(zsum.at[z_peer(-1)], near.at[0], r_ssem.at[4], r_rsem.at[4], chip(-1)))
        act(remote(zsum.at[z_peer(1)], near.at[1], r_ssem.at[5], r_rsem.at[5], chip(1)))

    def stage_two(act):
        act(remote(relay.at[0], twos.at[0], r_ssem.at[6], r_rsem.at[6], chip(-2)))
        act(remote(relay.at[1], twos.at[1], r_ssem.at[7], r_rsem.at[7], chip(2)))

    def arrived(index, slot):
        remote(slot, slot, r_ssem.at[index], r_rsem.at[index], partner).wait_recv()

    pl.when(z != 0)(produce)

    @pl.loop(1, nrow)
    def _(k):
        peer = row_peer(k)
        remote(gsend, gbuf.at[peer], g_ssem.at[k], g_rsem.at[peer], {"row": peer}).wait_recv()

    total = gbuf[0, 0:8]
    for r in range(1, nrow):
        total = total + gbuf[r, 0:8]
    table = (
        unpack(total, lanes)
        + jnp.where(lanes == rows + nb, 1.0, 0.0)
        + pltpu.roll(unpack(gbuf[0, 8:16], lanes), 2 * nb, 1)
    )
    (table,) = eliminate([table], nb)
    pivots = jnp.sum(jnp.where(lanes == rows, table, 0.0), axis=1, keepdims=True)
    table = table / jnp.sqrt(pivots)
    signs = jnp.sum(jnp.where(lanes == rows + 2 * nb, table, 0.0), axis=1, keepdims=True)
    flip = jnp.where(signs >= 0.0, -1.0, 1.0).astype(F32)
    upper = jnp.where((lanes >= rows) & (lanes < nb), table * flip, 0.0)
    correction = wide(upper[:, :nb].T)

    @pl.when(col == 0)
    def _():
        headbuf[...] = headbuf[...] - correction

    pl.when(z == 0)(produce)

    @pl.when(row == 0)
    def _():
        pt[:, 0:128] = pt[:, 0:128] - correction

    arrived(0, leaf3.at[0])
    arrived(2, leaf4.at[0])
    low_side = zsum[z_peer(-2)] + leaf3[0]
    relay[0, :, 0:half] = low_side[:, 0:half] + leaf4[0]
    relay[0, :, half:] = low_side[:, half:]
    arrived(1, leaf3.at[1])
    arrived(3, leaf4.at[1])
    high_side = zsum[z_peer(2)] + leaf3[1]
    relay[1, :, 0:half] = high_side[:, 0:half]
    relay[1, :, half:] = high_side[:, half:] + leaf4[1]
    stage_two(lambda copy: copy.start())

    load_f.wait()
    inner = cross(fv[...], pt[:, own_columns])
    for g in range(nz):
        columns = pl.ds(pl.multiple_of((core * nz + g) * chunk, chunk), chunk)
        inner = inner + cross(zsum[g], pt[:, columns])
    h1send[...] = pack(wide(inner))
    h1buf[row] = h1send[...]

    @pl.loop(1, nrow)
    def _(k):
        remote(h1send, h1buf.at[row], h1_ssem.at[k], h1_rsem.at[row], {"row": row_peer(k)}).start()

    @pl.when(row == 0)
    def _():
        extra = pltpu.make_async_copy(far.at[:, head_columns], obuf, load_sem.at[4])
        extra.start()
        head = sv.shape[1] * ncol
        ph, plow = split(pt[:, 0:head])
        sh, sl = split(sv[0:head, :])
        both = narrow(jnp.concatenate([ph, plow], 0), sh, NN)
        product = both[:nb] + both[nb:] + narrow(ph, sl, NN)
        extra.wait()
        osend[...] = product + obuf[...]
        obuf[...] = osend[...]

        @pl.loop(1, nrow)
        def _(k):
            remote(osend, obuf, o_ssem.at[k], o_rsem, {"row": row_peer(k)}).start()

    flipped_inverse = (pltpu.roll(table, 128 - nb, 1) * flip)[:, :nb]
    shifted_t = jnp.where(lanes == rows, 1.0, 0.0) - jnp.where(
        lanes < nb, pltpu.roll(table, 128 - 2 * nb, 1) * flip, 0.0
    )
    shifted = wide(shifted_t[:, :nb].T)
    augment = jnp.where(lanes == rows + nb, 1.0, 0.0)
    lower_table, upper_table = eliminate([shifted + augment, shifted_t + augment], nb)
    diagonal = jnp.sum(jnp.where(lanes == rows, upper_table, 0.0), axis=1, keepdims=True)
    lower_inverse = pltpu.roll(lower_table, 128 - nb, 1)[:, :nb]
    upper_inverse_t = (pltpu.roll(upper_table, 128 - nb, 1) / diagonal)[:, :nb]
    mixing_t = -exact(upper_inverse_t, flipped_inverse)
    second_t = -exact(lower_inverse, flipped_inverse)

    @pl.loop(1, nrow)
    def _(k):
        peer = row_peer(k)
        remote(h1send, h1buf.at[peer], h1_ssem.at[k], h1_rsem.at[peer], {"row": peer}).wait_recv()

    share = h1buf[0]
    for r in range(1, nrow):
        share = share + h1buf[r]
    h2send[...] = share
    h2buf[col] = share

    arrived(4, near.at[0])
    arrived(5, near.at[1])
    arrived(6, twos.at[0])
    arrived(7, twos.at[1])
    zown[...] = (fv[...] + zsum[z]) + (near[0] + near[1]) + (twos[0] + twos[1])

    @pl.loop(1, ncol)
    def _(k):
        remote(h2send, h2buf.at[col], h2_ssem.at[k], h2_rsem.at[col], {"col": col_peer(k)}).start()

    def slot(k):
        return images.at[core * nz + z_peer(k)]

    def half_slot(k, part):
        return images.at[core * nz + z_peer(k), :, pl.ds(part * half, half)]

    def gather(k):
        return remote(zown, slot(0), a_ssem.at[k % 8], a_rsem.at[-k % 8], chip(k))

    def got(k):
        remote(slot(k), slot(k), a_ssem.at[0], a_rsem.at[k % 8], partner).wait_recv()

    def got_half(part):
        remote(half_slot(4, part), half_slot(4, part), a_ssem.at[0], a_rsem.at[4 * part], partner).wait_recv()

    def pass_on():
        return (
            remote(slot(-2), slot(-2), a_ssem.at[3], a_rsem.at[5], chip(1)),
            remote(half_slot(-2, 0), half_slot(-2, 0), a_ssem.at[4], a_rsem.at[0], chip(2)),
            remote(slot(2), slot(2), a_ssem.at[5], a_rsem.at[3], chip(-1)),
            remote(half_slot(2, 1), half_slot(2, 1), a_ssem.at[0], a_rsem.at[4], chip(-2)),
        )

    def share_chunk(src, k):
        return remote(src, slot(k), f_ssem.at[z_peer(k)], f_rsem.at[z_peer(k)], partner)

    for k in (2, -2, 1, -1):
        gather(k).start()
    keep = pltpu.make_async_copy(zown, slot(0), image_sem)
    keep.start()
    share_chunk(zown, 0).start()
    copies = pass_on()
    got(-2)
    copies[0].start()
    copies[1].start()
    share_chunk(slot(-2), -2).start()
    got(2)
    copies[2].start()
    copies[3].start()
    share_chunk(slot(2), 2).start()
    for k in (1, -1):
        got(k)
        share_chunk(slot(k), k).start()

    own_reflectors = exact(mixing_t, headbuf[...])
    bottom = exact(second_t, own_reflectors, TN)
    kernel_t = exact(second_t, mixing_t, TN)

    @pl.when(row != 0)
    def _():
        remote(osend, obuf, o_ssem.at[0], o_rsem, {"row": 0}).wait_recv()

    own_base = exact(second_t, obuf[...])

    @pl.loop(1, ncol)
    def _(k):
        peer = col_peer(k)
        remote(h2send, h2buf.at[peer], h2_ssem.at[k], h2_rsem.at[peer], {"col": peer}).wait_recv()

    inner_total = h2buf[0]
    for c in range(1, ncol):
        inner_total = inner_total + h2buf[c]
    inner_t = unpack(inner_total, lanes)[:, :nb]
    weight_t = -0.5 * exact(exact(second_t, inner_t), kernel_t)
    own_weights = own_base + exact(weight_t, headbuf[...])
    top_part = exact(mixing_t, own_weights, TN) + exact(weight_t, own_reflectors, TN)
    coefs[0:nb, :] = top_part
    coefs[nb : 2 * nb, :] = bottom
    coefs[2 * nb : 3 * nb, :] = wide(jnp.concatenate([weight_t, second_t], 1))
    coefs[3 * nb :, :] = jnp.where(row == 0, correction, 0.0)

    for k in (3, -3):
        got(k)
        share_chunk(slot(k), k).start()
    got_half(0)
    got_half(1)
    share_chunk(slot(4), 4).start()

    @pl.loop(0, nz)
    def _(k):
        there = images.at[(1 - core) * nz + k]
        remote(there, there, f_ssem.at[k], f_rsem.at[k], partner).wait_recv()

    keep.wait()

    @pl.loop(0, nz)
    def _(k):
        remote(zout.at[k], pbuf.at[k], p_ssem.at[k], p_rsem.at[k], partner).wait_send()
        there = images.at[core * nz + k]
        remote(there, there, f_ssem.at[k], f_rsem.at[k], partner).wait_send()

    stage_one(lambda copy: copy.wait_send())
    stage_two(lambda copy: copy.wait_send())
    for k in (2, -2, 1, -1):
        gather(k).wait_send()
    for copy in copies:
        copy.wait_send()

    @pl.loop(1, nrow)
    def _(k):
        device = {"row": row_peer(k)}
        remote(gsend, gbuf.at[row], g_ssem.at[k], g_rsem.at[row], device).wait_send()
        remote(h1send, h1buf.at[row], h1_ssem.at[k], h1_rsem.at[row], device).wait_send()

    @pl.loop(1, ncol)
    def _(k):
        remote(h2send, h2buf.at[col], h2_ssem.at[k], h2_rsem.at[col], {"col": col_peer(k)}).wait_send()

    @pl.when(row == 0)
    def _():
        @pl.loop(1, nrow)
        def _(k):
            device = {"row": row_peer(k)}
            remote(pv.at[:, head_columns], headbuf, t_ssem.at[k], t_rsem, device).wait_send()
            remote(osend, obuf, o_ssem.at[k], o_rsem, device).wait_send()


def update_kernel(groups, slab, panel, images, coefs, updated, factor,
                  sv, pv, zv, cv, uv, wv, in_sem, coef_sem, out_sem):
    nb = 32
    parts = images.shape[0] // groups
    chunk = images.shape[2]
    length = parts * chunk

    def reads(g):
        span = pl.ds(pl.multiple_of(g * length, length), length)
        zs = pl.ds(g * parts, parts)
        return (
            pltpu.make_async_copy(panel.at[:, span], pv.at[:, span], in_sem.at[0, g]),
            pltpu.make_async_copy(images.at[zs], zv.at[zs], in_sem.at[1, g]),
            pltpu.make_async_copy(slab.at[span, :], sv.at[span, :], in_sem.at[2, g]),
        )

    def writes(g):
        span = pl.ds(pl.multiple_of(g * length, length), length)
        return (
            pltpu.make_async_copy(wv.at[:, span], factor.at[:, span], out_sem.at[0, g]),
            pltpu.make_async_copy(uv.at[span, :], updated.at[span, :], out_sem.at[1, g]),
        )

    load_c = pltpu.make_async_copy(coefs, cv, coef_sem)
    load_c.start()
    for g in range(groups):
        for copy in reads(g):
            copy.start()
    load_c.wait()
    bh, bl = split(cv[0 : 2 * nb, :])
    right = jnp.concatenate([bh, bl, bh], 0)
    ch, cl = split(cv[2 * nb : 3 * nb, 0 : 2 * nb])
    left = jnp.concatenate([ch, ch, cl], 1)
    for g in range(groups):
        for copy in reads(g):
            copy.wait()
        if g == 0:
            pv[:, 0:128] = pv[:, 0:128] - cv[3 * nb :, :]
        for i in range(g * parts, (g + 1) * parts):
            piece = slice(i * chunk, (i + 1) * chunk)
            xh, xl = split(jnp.concatenate([pv[:, piece], zv[i]], 0))
            wv[:, piece] = narrow(left, jnp.concatenate([xh, xl, xh], 0), NN)
            uv[piece, :] = sv[piece, :] - narrow(jnp.concatenate([xh, xh, xl], 0), right, TN)
        for copy in writes(g):
            copy.start()
    for g in range(groups):
        for copy in writes(g):
            copy.wait()


def local(nrow, ncol, slab, panel, far):
    nb, length = panel.shape
    chunk = length // ncol
    nz = ncol // 2
    anywhere = pl.BlockSpec(memory_space=pl.ANY)
    vmem = pl.BlockSpec(memory_space=pltpu.VMEM)
    dma = pltpu.SemaphoreType.DMA
    strip = pltpu.VMEM((nb, 128), F32)
    tile = pltpu.VMEM((8, 128), F32)

    def chunks(n, width=chunk):
        return pltpu.VMEM((n, nb, width), F32)

    images, coefs = pl.pallas_call(
        functools.partial(exchange_kernel, nrow, ncol),
        name="exchange",
        out_shape=(
            jax.ShapeDtypeStruct((ncol, nb, chunk), F32),
            jax.ShapeDtypeStruct((4 * nb, 128), F32),
        ),
        in_specs=[anywhere] * 3,
        out_specs=(anywhere, vmem),
        scratch_shapes=[
            pltpu.VMEM((nb, length), F32),
            pltpu.VMEM(slab.shape, F32),
            pltpu.VMEM((nb, chunk), F32),
            pltpu.VMEM((16, 128), F32),
            pltpu.VMEM((nrow, 16, 128), F32),
            strip,
            pltpu.VMEM((nb, length), F32),
            chunks(nz), chunks(nz), chunks(nz),
            chunks(2), chunks(2, chunk // 2), chunks(2), chunks(2), chunks(2),
            pltpu.VMEM((nb, chunk), F32),
            strip, strip,
            tile, pltpu.VMEM((nrow, 8, 128), F32),
            tile, pltpu.VMEM((ncol, 8, 128), F32),
            dma((5,)),
            dma((nrow,)), dma((nrow,)),
            dma((nrow,)), dma(()),
            dma((nz,)), dma((nz,)),
            dma((8,)), dma((8,)),
            dma((8,)), dma((8,)),
            dma((nz,)), dma((nz,)),
            dma((nrow,)), dma(()),
            dma((nrow,)), dma((nrow,)),
            dma((ncol,)), dma((ncol,)),
            dma(()),
        ],
        compiler_params=pltpu.CompilerParams(
            collective_id=0, has_side_effects=True, vmem_limit_bytes=60 * 2**20
        ),
    )(slab, panel, far)
    groups = 8
    return pl.pallas_call(
        functools.partial(update_kernel, groups),
        name="update",
        out_shape=(
            jax.ShapeDtypeStruct(slab.shape, F32),
            jax.ShapeDtypeStruct(panel.shape, F32),
        ),
        in_specs=[anywhere] * 4,
        out_specs=(anywhere, anywhere),
        scratch_shapes=[
            pltpu.VMEM(slab.shape, F32),
            pltpu.VMEM(panel.shape, F32),
            pltpu.VMEM((ncol, nb, chunk), F32),
            pltpu.VMEM((4 * nb, 128), F32),
            pltpu.VMEM(slab.shape, F32),
            pltpu.VMEM(panel.shape, F32),
            dma((3, groups)), dma(()), dma((2, groups)),
        ],
        compiler_params=pltpu.CompilerParams(vmem_limit_bytes=60 * 2**20),
    )(slab, panel, images, coefs)


def solution(mesh):
    sizes = dict(mesh.shape)
    body = functools.partial(local, sizes["row"], sizes["col"])
    in_specs = (P("row", "col"), P(None, "row"), P(None, "row"))
    out_specs = (P("row", "col"), P(None, "row"))
    return jax.shard_map(body, mesh=mesh, in_specs=in_specs, out_specs=out_specs, check_vma=False)
```

```python
import functools

import jax
import jax.numpy as jnp
from jax import lax
from jax.experimental import pallas as pl
from jax.experimental.pallas import tpu as pltpu
from jax.sharding import PartitionSpec as P

F32 = jnp.float32
BF16 = jnp.bfloat16
MESH = pl.DeviceIdType.MESH
NT = (((1,), (1,)), ((), ()))
TN = (((0,), (0,)), ((), ()))
NN = (((1,), (0,)), ((), ()))


def exact(left, right, dims=NN):
    return lax.dot_general(
        left, right, dims, precision=lax.Precision.HIGHEST, preferred_element_type=F32
    )


def narrow(left, right, dims):
    return lax.dot_general(left, right, dims, preferred_element_type=F32)


def split(x):
    high = x.astype(BF16)
    low = (x - high.astype(F32)).astype(BF16)
    return high, low


def split3(x):
    high = x.astype(BF16)
    rest = x - high.astype(F32)
    mid = rest.astype(BF16)
    low = (rest - mid.astype(F32)).astype(BF16)
    return high, mid, low


def gram_of(block):
    nb = block.shape[0]
    one, two, three = split3(block)
    first = narrow(jnp.concatenate([one, two, three], 0), one, NT)
    second = narrow(jnp.concatenate([one, two], 0), two, NT)
    third = narrow(one, three, NT)
    return (
        first[:nb]
        + (first[nb : 2 * nb] + second[:nb])
        + (first[2 * nb :] + second[nb:] + third)
    )


def cross(left, right):
    nb = left.shape[0]
    lh, ll = split(left)
    rh, rl = split(right)
    both = narrow(jnp.concatenate([lh, ll], 0), rh, NT)
    return both[:nb] + both[nb:] + narrow(lh, rl, NT)


def eliminate(tables, nb):
    rows = lax.broadcasted_iota(jnp.int32, (nb, 128), 0)
    for j in range(nb):
        done = []
        for table in tables:
            column = jnp.broadcast_to(table[:, j : j + 1], (nb, 128))
            pivot_row = table[j : j + 1, :] / column[j : j + 1, :]
            done.append(table - jnp.where(rows > j, column, 0.0) * pivot_row)
        tables = done
    return tables


def pack(square):
    total = square[0:8]
    for k in range(1, 4):
        total = total + pltpu.roll(square[8 * k : 8 * k + 8], 32 * k, 1)
    return total


def unpack(packed, lanes):
    parts = [packed] + [pltpu.roll(packed, 128 - 32 * k, 1) for k in range(1, 4)]
    return jnp.where(lanes < 32, jnp.concatenate(parts, 0), 0.0)


def wide(square):
    return jnp.concatenate([square, jnp.zeros((square.shape[0], 128 - square.shape[1]), F32)], 1)


def exchange_kernel(
    nrow, ncol,
    slab, panel, far,
    images, coefs,
    pv, sv, fv, gsend, gbuf, headbuf, pt, zout, pbuf, zsum,
    leaf3, leaf4, near, relay, twos, zown, osend, obuf, h1send, h1buf, h2send, h2buf,
    load_sem, g_ssem, g_rsem, t_ssem, t_rsem, p_ssem, p_rsem, r_ssem, r_rsem,
    a_ssem, a_rsem, f_ssem, f_rsem, o_ssem, o_rsem, h1_ssem, h1_rsem, h2_ssem, h2_rsem,
    image_sem,
):
    nb = 32
    nz = ncol // 2
    chunk = pv.shape[1] // ncol
    half = chunk // 2
    row = lax.axis_index("row")
    col = lax.axis_index("col")
    z = lax.div(col, 2)
    core = lax.rem(col, 2)
    partner = {"col": col + 1 - 2 * core}
    rows = lax.broadcasted_iota(jnp.int32, (nb, 128), 0)
    lanes = lax.broadcasted_iota(jnp.int32, (nb, 128), 1)

    def remote(src, dst, ssem, rsem, device):
        return pltpu.make_async_remote_copy(
            src_ref=src, dst_ref=dst, send_sem=ssem, recv_sem=rsem,
            device_id=device, device_id_type=MESH,
        )

    def others(buffer, n, ssem, rsem):
        slots = buffer.at[pl.ds(0, n - 1)]
        return remote(slots, slots, ssem, rsem, partner)

    def row_peer(k):
        return lax.rem(row + k, nrow)

    def col_peer(k):
        return lax.rem(col + k, ncol)

    def z_peer(k):
        return lax.rem(z + k + nz, nz)

    def chip(k):
        return {"col": 2 * z_peer(k) + core}

    load_p = pltpu.make_async_copy(panel, pv, load_sem.at[0])
    load_s = pltpu.make_async_copy(slab, sv, load_sem.at[1])
    own = core * nz + z
    own_columns = pl.ds(pl.multiple_of(own * chunk, chunk), chunk)
    load_f = pltpu.make_async_copy(far.at[:, own_columns], fv, load_sem.at[2])
    load_p.start()
    load_s.start()
    load_f.start()

    barrier = pltpu.get_barrier_semaphore()

    @pl.loop(1, nrow)
    def _(k):
        pl.semaphore_signal(barrier, inc=1, device_id={"row": row_peer(k)}, device_id_type=MESH)

    for device in (partner, chip(1), chip(-1), chip(2), chip(-2)):
        pl.semaphore_signal(barrier, inc=1, device_id=device, device_id_type=MESH)

    load_p.wait()
    gram = jnp.zeros((nb, nb), F32)
    for g in range(ncol):
        gram = gram + gram_of(pv[:, g * chunk : (g + 1) * chunk])
    gsend[0:8, :] = pack(wide(gram))
    gsend[8:16, :] = pack(jnp.where(lanes < nb, pv[:, 0:128], 0.0))
    gbuf[row] = gsend[...]
    pt[...] = pv[...]
    pl.semaphore_wait(barrier, nrow + 4)

    head_columns = pl.ds(pl.multiple_of(col * 128, 128), 128)

    @pl.when(row == 0)
    def _():
        for k in range(1, nrow):
            remote(pv.at[:, head_columns], headbuf, t_ssem, t_rsem, {"row": row_peer(k)}).start()

    for k in range(1, nrow):
        remote(gsend, gbuf.at[row], g_ssem, g_rsem, {"row": row_peer(k)}).start()

    @pl.when(row == 0)
    def _():
        local_head = pltpu.make_async_copy(pv.at[:, head_columns], headbuf, load_sem.at[3])
        local_head.start()
        local_head.wait()

    load_s.wait()

    @pl.when(row != 0)
    def _():
        remote(headbuf, headbuf, t_ssem, t_rsem, {"row": 0}).wait_recv()

    def produce():
        high, low = split(headbuf[...])
        weights = jnp.concatenate(
            [
                jnp.concatenate([high, high], 1),
                jnp.concatenate([low, jnp.zeros_like(low)], 1),
            ],
            0,
        )

        def product(index):
            block = sv[pl.ds(pl.multiple_of(index * chunk, chunk), chunk), :]
            sh, sl = split(block)
            both = narrow(weights, jnp.concatenate([sh, sl], 1), NT)
            return both[:nb] + both[nb:]

        def to_partner(peer):
            return remote(zout.at[peer], pbuf.at[peer], p_ssem, p_rsem.at[peer], partner)

        def other_half(k):
            peer = z_peer(k)
            zout[peer] = product((1 - core) * nz + peer)

            @pl.when(k > 3)
            def _():
                to_partner(z_peer(k - 1)).start()

        def own_half(k):
            peer = z_peer(k)
            part = product(core * nz + peer)
            to_partner(peer).wait_recv()
            zsum[peer] = part + pbuf[peer]

        pl.loop(3, nz + 3)(other_half)
        to_partner(z_peer(nz + 2)).start()
        pl.loop(3, nz - 2)(own_half)
        pl.loop(nz - 2, nz + 3)(own_half)
        stage_one(lambda copy: copy.start())

    def stage_one(act):
        act(remote(zsum.at[z_peer(-3)], leaf3.at[0], r_ssem.at[0], r_rsem.at[0], chip(-1)))
        act(remote(zsum.at[z_peer(3)], leaf3.at[1], r_ssem.at[1], r_rsem.at[1], chip(1)))
        first = zsum.at[z_peer(4), :, pl.ds(0, half)]
        second = zsum.at[z_peer(4), :, pl.ds(half, half)]
        act(remote(first, leaf4.at[0], r_ssem.at[2], r_rsem.at[2], chip(-2)))
        act(remote(second, leaf4.at[1], r_ssem.at[3], r_rsem.at[3], chip(2)))
        act(remote(zsum.at[z_peer(-1)], near.at[0], r_ssem.at[4], r_rsem.at[4], chip(-1)))
        act(remote(zsum.at[z_peer(1)], near.at[1], r_ssem.at[5], r_rsem.at[5], chip(1)))

    def stage_two(act):
        act(remote(relay.at[0], twos.at[0], r_ssem.at[6], r_rsem.at[6], chip(-2)))
        act(remote(relay.at[1], twos.at[1], r_ssem.at[7], r_rsem.at[7], chip(2)))

    def arrived(index, slot):
        remote(slot, slot, r_ssem.at[index], r_rsem.at[index], partner).wait_recv()

    pl.when(z != 0)(produce)

    others(gbuf, nrow, g_ssem, g_rsem).wait_recv()

    total = gbuf[0, 0:8]
    for r in range(1, nrow):
        total = total + gbuf[r, 0:8]
    table = (
        unpack(total, lanes)
        + jnp.where(lanes == rows + nb, 1.0, 0.0)
        + pltpu.roll(unpack(gbuf[0, 8:16], lanes), 2 * nb, 1)
    )
    (table,) = eliminate([table], nb)
    pivots = jnp.sum(jnp.where(lanes == rows, table, 0.0), axis=1, keepdims=True)
    table = table / jnp.sqrt(pivots)
    signs = jnp.sum(jnp.where(lanes == rows + 2 * nb, table, 0.0), axis=1, keepdims=True)
    flip = jnp.where(signs >= 0.0, -1.0, 1.0).astype(F32)
    upper = jnp.where((lanes >= rows) & (lanes < nb), table * flip, 0.0)
    correction = wide(upper[:, :nb].T)

    @pl.when(col == 0)
    def _():
        headbuf[...] = headbuf[...] - correction

    pl.when(z == 0)(produce)

    @pl.when(row == 0)
    def _():
        pt[:, 0:128] = pt[:, 0:128] - correction

    arrived(0, leaf3.at[0])
    arrived(2, leaf4.at[0])
    low_side = zsum[z_peer(-2)] + leaf3[0]
    relay[0, :, 0:half] = low_side[:, 0:half] + leaf4[0]
    relay[0, :, half:] = low_side[:, half:]
    arrived(1, leaf3.at[1])
    arrived(3, leaf4.at[1])
    high_side = zsum[z_peer(2)] + leaf3[1]
    relay[1, :, 0:half] = high_side[:, 0:half]
    relay[1, :, half:] = high_side[:, half:] + leaf4[1]
    stage_two(lambda copy: copy.start())

    load_f.wait()
    inner = cross(fv[...], pt[:, own_columns])
    for g in range(nz):
        columns = pl.ds(pl.multiple_of((core * nz + g) * chunk, chunk), chunk)
        inner = inner + cross(zsum[g], pt[:, columns])
    h1send[...] = pack(wide(inner))
    h1buf[row] = h1send[...]

    for k in range(1, nrow):
        remote(h1send, h1buf.at[row], h1_ssem, h1_rsem, {"row": row_peer(k)}).start()

    @pl.when(row == 0)
    def _():
        extra = pltpu.make_async_copy(far.at[:, head_columns], obuf, load_sem.at[4])
        extra.start()
        head = sv.shape[1] * ncol
        ph, plow = split(pt[:, 0:head])
        sh, sl = split(sv[0:head, :])
        both = narrow(jnp.concatenate([ph, plow], 0), sh, NN)
        product = both[:nb] + both[nb:] + narrow(ph, sl, NN)
        extra.wait()
        osend[...] = product + obuf[...]
        obuf[...] = osend[...]

        for k in range(1, nrow):
            remote(osend, obuf, o_ssem, o_rsem, {"row": row_peer(k)}).start()

    flipped_inverse = (pltpu.roll(table, 128 - nb, 1) * flip)[:, :nb]
    shifted_t = jnp.where(lanes == rows, 1.0, 0.0) - jnp.where(
        lanes < nb, pltpu.roll(table, 128 - 2 * nb, 1) * flip, 0.0
    )
    shifted = wide(shifted_t[:, :nb].T)
    augment = jnp.where(lanes == rows + nb, 1.0, 0.0)
    lower_table, upper_table = eliminate([shifted + augment, shifted_t + augment], nb)
    diagonal = jnp.sum(jnp.where(lanes == rows, upper_table, 0.0), axis=1, keepdims=True)
    lower_inverse = pltpu.roll(lower_table, 128 - nb, 1)[:, :nb]
    upper_inverse_t = (pltpu.roll(upper_table, 128 - nb, 1) / diagonal)[:, :nb]
    mixing_t = -exact(upper_inverse_t, flipped_inverse)
    second_t = -exact(lower_inverse, flipped_inverse)

    others(h1buf, nrow, h1_ssem, h1_rsem).wait_recv()

    share = h1buf[0]
    for r in range(1, nrow):
        share = share + h1buf[r]
    h2send[...] = share
    h2buf[col] = share

    arrived(4, near.at[0])
    arrived(5, near.at[1])
    arrived(6, twos.at[0])
    arrived(7, twos.at[1])
    zown[...] = (fv[...] + zsum[z]) + (near[0] + near[1]) + (twos[0] + twos[1])

    for k in range(1, ncol):
        remote(h2send, h2buf.at[col], h2_ssem, h2_rsem, {"col": col_peer(k)}).start()

    def slot(k):
        return images.at[core * nz + z_peer(k)]

    def half_slot(k, part):
        return images.at[core * nz + z_peer(k), :, pl.ds(part * half, half)]

    def gather(k):
        return remote(zown, slot(0), a_ssem.at[k % 8], a_rsem.at[-k % 8], chip(k))

    def got(k):
        remote(slot(k), slot(k), a_ssem.at[0], a_rsem.at[k % 8], partner).wait_recv()

    def got_half(part):
        remote(half_slot(4, part), half_slot(4, part), a_ssem.at[0], a_rsem.at[4 * part], partner).wait_recv()

    def pass_on():
        return (
            remote(slot(-2), slot(-2), a_ssem.at[3], a_rsem.at[5], chip(1)),
            remote(half_slot(-2, 0), half_slot(-2, 0), a_ssem.at[4], a_rsem.at[0], chip(2)),
            remote(slot(2), slot(2), a_ssem.at[5], a_rsem.at[3], chip(-1)),
            remote(half_slot(2, 1), half_slot(2, 1), a_ssem.at[0], a_rsem.at[4], chip(-2)),
        )

    def share_chunk(src, k):
        return remote(src, slot(k), f_ssem, f_rsem, partner)

    for k in (2, -2, 1, -1):
        gather(k).start()
    keep = pltpu.make_async_copy(zown, slot(0), image_sem)
    keep.start()
    share_chunk(zown, 0).start()
    copies = pass_on()
    got(-2)
    copies[0].start()
    copies[1].start()
    share_chunk(slot(-2), -2).start()
    got(2)
    copies[2].start()
    copies[3].start()
    share_chunk(slot(2), 2).start()
    for k in (1, -1):
        got(k)
        share_chunk(slot(k), k).start()

    own_reflectors = exact(mixing_t, headbuf[...])
    bottom = exact(second_t, own_reflectors, TN)
    kernel_t = exact(second_t, mixing_t, TN)

    @pl.when(row != 0)
    def _():
        remote(obuf, obuf, o_ssem, o_rsem, {"row": 0}).wait_recv()

    own_base = exact(second_t, obuf[...])

    others(h2buf, ncol, h2_ssem, h2_rsem).wait_recv()

    inner_total = h2buf[0]
    for c in range(1, ncol):
        inner_total = inner_total + h2buf[c]
    inner_t = unpack(inner_total, lanes)[:, :nb]
    weight_t = -0.5 * exact(exact(second_t, inner_t), kernel_t)
    own_weights = own_base + exact(weight_t, headbuf[...])
    top_part = exact(mixing_t, own_weights, TN) + exact(weight_t, own_reflectors, TN)
    coefs[0:nb, :] = top_part
    coefs[nb : 2 * nb, :] = bottom
    coefs[2 * nb : 3 * nb, :] = wide(jnp.concatenate([weight_t, second_t], 1))
    coefs[3 * nb :, :] = jnp.where(row == 0, correction, 0.0)

    for k in (3, -3):
        got(k)
        share_chunk(slot(k), k).start()
    got_half(0)
    got_half(1)
    share_chunk(slot(4), 4).start()

    theirs = images.at[pl.ds((1 - core) * nz, nz)]
    remote(theirs, theirs, f_ssem, f_rsem, partner).wait_recv()

    keep.wait()

    remote(zout, pbuf, p_ssem, p_rsem.at[0], partner).wait_send()
    mine = images.at[pl.ds(0, nz)]
    remote(mine, mine, f_ssem, f_rsem, partner).wait_send()
    stage_one(lambda copy: copy.wait_send())
    stage_two(lambda copy: copy.wait_send())
    for k in (2, -2, 1, -1):
        gather(k).wait_send()
    for copy in copies:
        copy.wait_send()
    others(gbuf, nrow, g_ssem, g_rsem).wait_send()
    others(h1buf, nrow, h1_ssem, h1_rsem).wait_send()
    others(h2buf, ncol, h2_ssem, h2_rsem).wait_send()

    @pl.when(row == 0)
    def _():
        heads = pv.at[:, pl.ds(0, 128 * (nrow - 1))]
        remote(heads, heads, t_ssem, t_rsem, partner).wait_send()
        remote(heads, heads, o_ssem, o_rsem, partner).wait_send()


def update_kernel(groups, slab, panel, images, coefs, updated, factor, uv, wv, out_sem):
    nb = 32
    parts = images.shape[0] // groups
    chunk = images.shape[2]
    length = parts * chunk

    def writes(g):
        span = pl.ds(g * length, length)
        return (
            pltpu.make_async_copy(wv.at[:, span], factor.at[:, span], out_sem.at[0, g]),
            pltpu.make_async_copy(uv.at[span, :], updated.at[span, :], out_sem.at[1, g]),
        )

    bh, bl = split(coefs[0 : 2 * nb, :])
    right = jnp.concatenate([bh, bl, bh], 0)
    ch, cl = split(coefs[2 * nb : 3 * nb, 0 : 2 * nb])
    left = jnp.concatenate([ch, ch, cl], 1)
    for g in range(groups):
        for i in range(g * parts, (g + 1) * parts):
            piece = slice(i * chunk, (i + 1) * chunk)
            columns = panel[:, piece]
            if i == 0:
                columns = jnp.concatenate(
                    [columns[:, 0:128] - coefs[3 * nb :, :], columns[:, 128:]], 1
                )
            xh, xl = split(jnp.concatenate([columns, images[i]], 0))
            wv[:, piece] = narrow(left, jnp.concatenate([xh, xl, xh], 0), NN)
            uv[piece, :] = slab[piece, :] - narrow(jnp.concatenate([xh, xh, xl], 0), right, TN)
        for copy in writes(g):
            copy.start()
    for g in range(groups):
        for copy in writes(g):
            copy.wait()


def local(nrow, ncol, slab, panel, far):
    nb, length = panel.shape
    chunk = length // ncol
    nz = ncol // 2
    anywhere = pl.BlockSpec(memory_space=pl.ANY)
    vmem = pl.BlockSpec(memory_space=pltpu.VMEM)
    dma = pltpu.SemaphoreType.DMA
    strip = pltpu.VMEM((nb, 128), F32)
    tile = pltpu.VMEM((8, 128), F32)

    def chunks(n, width=chunk):
        return pltpu.VMEM((n, nb, width), F32)

    images, coefs = pl.pallas_call(
        functools.partial(exchange_kernel, nrow, ncol),
        name="exchange",
        out_shape=(
            jax.ShapeDtypeStruct((ncol, nb, chunk), F32),
            jax.ShapeDtypeStruct((4 * nb, 128), F32),
        ),
        in_specs=[anywhere] * 3,
        out_specs=(anywhere, vmem),
        scratch_shapes=[
            pltpu.VMEM((nb, length), F32),
            pltpu.VMEM(slab.shape, F32),
            pltpu.VMEM((nb, chunk), F32),
            pltpu.VMEM((16, 128), F32),
            pltpu.VMEM((nrow, 16, 128), F32),
            strip,
            pltpu.VMEM((nb, length), F32),
            chunks(nz), chunks(nz), chunks(nz),
            chunks(2), chunks(2, chunk // 2), chunks(2), chunks(2), chunks(2),
            pltpu.VMEM((nb, chunk), F32),
            strip, strip,
            tile, pltpu.VMEM((nrow, 8, 128), F32),
            tile, pltpu.VMEM((ncol, 8, 128), F32),
            dma((5,)),
            dma(()), dma(()),
            dma(()), dma(()),
            dma(()), dma((nz,)),
            dma((8,)), dma((8,)),
            dma((8,)), dma((8,)),
            dma(()), dma(()),
            dma(()), dma(()),
            dma(()), dma(()),
            dma(()), dma(()),
            dma(()),
        ],
        compiler_params=pltpu.CompilerParams(
            collective_id=0, has_side_effects=True, vmem_limit_bytes=24 * 2**20
        ),
    )(*(pltpu.with_memory_space_constraint(array, pltpu.HBM) for array in (slab, panel, far)))
    groups = 4
    return pl.pallas_call(
        functools.partial(update_kernel, groups),
        name="update",
        out_shape=(
            jax.ShapeDtypeStruct(slab.shape, F32),
            jax.ShapeDtypeStruct(panel.shape, F32),
        ),
        in_specs=[vmem] * 4,
        out_specs=(anywhere, anywhere),
        scratch_shapes=[
            pltpu.VMEM(slab.shape, F32),
            pltpu.VMEM(panel.shape, F32),
            dma((2, groups)),
        ],
        compiler_params=pltpu.CompilerParams(vmem_limit_bytes=24 * 2**20),
    )(slab, panel, images, coefs)


def solution(mesh):
    sizes = dict(mesh.shape)
    body = functools.partial(local, sizes["row"], sizes["col"])
    in_specs = (P("row", "col"), P(None, "row"), P(None, "row"))
    out_specs = (P("row", "col"), P(None, "row"))
    return jax.shard_map(body, mesh=mesh, in_specs=in_specs, out_specs=out_specs, check_vma=False)
```

```python
import functools

import jax
import jax.numpy as jnp
from jax import lax
from jax.experimental import pallas as pl
from jax.experimental.pallas import tpu as pltpu
from jax.sharding import PartitionSpec as P

F32 = jnp.float32
BF16 = jnp.bfloat16
MESH = pl.DeviceIdType.MESH
NT = (((1,), (1,)), ((), ()))
TN = (((0,), (0,)), ((), ()))
NN = (((1,), (0,)), ((), ()))


def exact(left, right, dims=NN):
    return lax.dot_general(
        left, right, dims, precision=lax.Precision.HIGHEST, preferred_element_type=F32
    )


def narrow(left, right, dims):
    return lax.dot_general(left, right, dims, preferred_element_type=F32)


def split(x):
    high = x.astype(BF16)
    low = (x - high.astype(F32)).astype(BF16)
    return high, low


def split3(x):
    high = x.astype(BF16)
    rest = x - high.astype(F32)
    mid = rest.astype(BF16)
    low = (rest - mid.astype(F32)).astype(BF16)
    return high, mid, low


def gram_of(block):
    nb = block.shape[0]
    one, two, three = split3(block)
    first = narrow(jnp.concatenate([one, two, three], 0), one, NT)
    second = narrow(jnp.concatenate([one, two], 0), two, NT)
    third = narrow(one, three, NT)
    return (
        first[:nb]
        + (first[nb : 2 * nb] + second[:nb])
        + (first[2 * nb :] + second[nb:] + third)
    )


def cross(left, right):
    nb = left.shape[0]
    lh, ll = split(left)
    rh, rl = split(right)
    both = narrow(jnp.concatenate([lh, ll], 0), rh, NT)
    return both[:nb] + both[nb:] + narrow(lh, rl, NT)


def eliminate(tables, nb):
    rows = lax.broadcasted_iota(jnp.int32, (nb, 128), 0)
    for j in range(0, nb, 2):
        done = []
        for table in tables:
            column = jnp.broadcast_to(table[:, j : j + 1], (nb, 128))
            following = jnp.broadcast_to(table[:, j + 1 : j + 2], (nb, 128))
            pivot = column[j : j + 1, :]
            pivot_row = table[j : j + 1, :] / pivot
            below = jnp.where(rows > j, column, 0.0)
            following = following - below * (following[j : j + 1, :] / pivot)
            next_row = table[j + 1 : j + 2, :] - column[j + 1 : j + 2, :] * pivot_row
            next_row = next_row / following[j + 1 : j + 2, :]
            after = jnp.where(rows > j + 1, following, 0.0)
            done.append(table - below * pivot_row - after * next_row)
        tables = done
    return tables


def pack(square):
    total = square[0:8]
    for k in range(1, 4):
        total = total + pltpu.roll(square[8 * k : 8 * k + 8], 32 * k, 1)
    return total


def unpack(packed, lanes):
    parts = [packed] + [pltpu.roll(packed, 128 - 32 * k, 1) for k in range(1, 4)]
    return jnp.where(lanes < 32, jnp.concatenate(parts, 0), 0.0)


def wide(square):
    return jnp.concatenate([square, jnp.zeros((square.shape[0], 128 - square.shape[1]), F32)], 1)


def exchange_kernel(
    nrow, ncol,
    slab, panel, far,
    images, coefs,
    pv, sv, fv, gsend, gbuf, headbuf, pt, zout, pbuf, zsum,
    leaf3, leaf4, near, relay, twos, zown, osend, obuf, h1send, h1buf, h2send, h2buf, pairsend, pairbuf,
    load_sem, g_ssem, g_rsem, t_ssem, t_rsem, p_ssem, p_rsem, r_ssem, r_rsem,
    a_ssem, a_rsem, f_ssem, f_rsem, o_ssem, o_rsem, h1_ssem, h1_rsem, h2_ssem, h2_rsem,
    pair_sem, image_sem,
):
    nb = 32
    nz = ncol // 2
    chunk = pv.shape[1] // ncol
    half = chunk // 2
    row = lax.axis_index("row")
    col = lax.axis_index("col")
    z = lax.div(col, 2)
    core = lax.rem(col, 2)
    partner = {"col": col + 1 - 2 * core}
    rows = lax.broadcasted_iota(jnp.int32, (nb, 128), 0)
    lanes = lax.broadcasted_iota(jnp.int32, (nb, 128), 1)

    def remote(src, dst, ssem, rsem, device):
        return pltpu.make_async_remote_copy(
            src_ref=src, dst_ref=dst, send_sem=ssem, recv_sem=rsem,
            device_id=device, device_id_type=MESH,
        )

    def others(buffer, n, ssem, rsem):
        slots = buffer.at[pl.ds(0, n - 1)]
        return remote(slots, slots, ssem, rsem, partner)

    def row_peer(k):
        return lax.rem(row + k, nrow)

    def z_peer(k):
        return lax.rem(z + k + nz, nz)

    def chip(k):
        return {"col": 2 * z_peer(k) + core}

    load_p = pltpu.make_async_copy(panel, pv, load_sem.at[0])
    load_s = pltpu.make_async_copy(slab, sv, load_sem.at[1])
    own = core * nz + z
    own_columns = pl.ds(pl.multiple_of(own * chunk, chunk), chunk)
    load_f = pltpu.make_async_copy(far.at[:, own_columns], fv, load_sem.at[2])
    load_p.start()
    load_s.start()
    load_f.start()

    barrier = pltpu.get_barrier_semaphore()

    @pl.loop(1, nrow)
    def _(k):
        pl.semaphore_signal(barrier, inc=1, device_id={"row": row_peer(k)}, device_id_type=MESH)

    for device in (partner, chip(1), chip(-1), chip(2), chip(-2)):
        pl.semaphore_signal(barrier, inc=1, device_id=device, device_id_type=MESH)

    load_p.wait()
    gram = jnp.zeros((nb, nb), F32)
    for g in range(ncol):
        gram = gram + gram_of(pv[:, g * chunk : (g + 1) * chunk])
    gsend[0:8, :] = pack(wide(gram))
    gsend[8:16, :] = pack(jnp.where(lanes < nb, pv[:, 0:128], 0.0))
    gbuf[row] = gsend[...]
    pt[...] = pv[...]
    pl.semaphore_wait(barrier, nrow + 4)

    head_columns = pl.ds(pl.multiple_of(col * 128, 128), 128)

    @pl.when(row == 0)
    def _():
        for k in range(1, nrow):
            remote(pv.at[:, head_columns], headbuf, t_ssem, t_rsem, {"row": row_peer(k)}).start()

    for k in range(1, nrow):
        remote(gsend, gbuf.at[row], g_ssem, g_rsem, {"row": row_peer(k)}).start()

    @pl.when(row == 0)
    def _():
        local_head = pltpu.make_async_copy(pv.at[:, head_columns], headbuf, load_sem.at[3])
        local_head.start()
        local_head.wait()

    load_s.wait()

    @pl.when(row != 0)
    def _():
        remote(headbuf, headbuf, t_ssem, t_rsem, {"row": 0}).wait_recv()

    def produce():
        high, low = split(headbuf[...])
        weights = jnp.concatenate(
            [
                jnp.concatenate([high, high], 1),
                jnp.concatenate([low, jnp.zeros_like(low)], 1),
            ],
            0,
        )

        def product(index):
            block = sv[pl.ds(pl.multiple_of(index * chunk, chunk), chunk), :]
            sh, sl = split(block)
            both = narrow(weights, jnp.concatenate([sh, sl], 1), NT)
            return both[:nb] + both[nb:]

        def to_partner(peer):
            return remote(zout.at[peer], pbuf.at[peer], p_ssem, p_rsem.at[peer], partner)

        def other_half(k):
            peer = z_peer(k)
            zout[peer] = product((1 - core) * nz + peer)

            @pl.when(k > 3)
            def _():
                to_partner(z_peer(k - 1)).start()

        def own_half(k):
            peer = z_peer(k)
            part = product(core * nz + peer)
            to_partner(peer).wait_recv()
            zsum[peer] = part + pbuf[peer]

        pl.loop(3, nz)(other_half)
        pl.loop(3, nz - 2)(own_half)
        leaves(lambda copy: copy.start())
        pl.loop(nz, nz + 3)(other_half)
        to_partner(z_peer(nz + 2)).start()
        pl.loop(nz - 2, nz + 3)(own_half)
        nears(lambda copy: copy.start())

    def leaves(act):
        act(remote(zsum.at[z_peer(-3)], leaf3.at[0], r_ssem.at[0], r_rsem.at[0], chip(-1)))
        act(remote(zsum.at[z_peer(3)], leaf3.at[1], r_ssem.at[1], r_rsem.at[1], chip(1)))
        first = zsum.at[z_peer(4), :, pl.ds(0, half)]
        second = zsum.at[z_peer(4), :, pl.ds(half, half)]
        act(remote(first, leaf4.at[0], r_ssem.at[2], r_rsem.at[2], chip(-2)))
        act(remote(second, leaf4.at[1], r_ssem.at[3], r_rsem.at[3], chip(2)))

    def nears(act):
        act(remote(zsum.at[z_peer(-1)], near.at[0], r_ssem.at[4], r_rsem.at[4], chip(-1)))
        act(remote(zsum.at[z_peer(1)], near.at[1], r_ssem.at[5], r_rsem.at[5], chip(1)))

    def stage_two(act):
        act(remote(relay.at[0], twos.at[0], r_ssem.at[6], r_rsem.at[6], chip(-2)))
        act(remote(relay.at[1], twos.at[1], r_ssem.at[7], r_rsem.at[7], chip(2)))

    def arrived(index, slot):
        remote(slot, slot, r_ssem.at[index], r_rsem.at[index], partner).wait_recv()

    pl.when(z != 0)(produce)

    others(gbuf, nrow, g_ssem, g_rsem).wait_recv()

    total = gbuf[0, 0:8]
    for r in range(1, nrow):
        total = total + gbuf[r, 0:8]
    table = (
        unpack(total, lanes)
        + jnp.where(lanes == rows + nb, 1.0, 0.0)
        + pltpu.roll(unpack(gbuf[0, 8:16], lanes), 2 * nb, 1)
    )
    (table,) = eliminate([table], nb)
    pivots = jnp.sum(jnp.where(lanes == rows, table, 0.0), axis=1, keepdims=True)
    table = table / jnp.sqrt(pivots)
    signs = jnp.sum(jnp.where(lanes == rows + 2 * nb, table, 0.0), axis=1, keepdims=True)
    flip = jnp.where(signs >= 0.0, -1.0, 1.0).astype(F32)
    upper = jnp.where((lanes >= rows) & (lanes < nb), table * flip, 0.0)
    correction = wide(upper[:, :nb].T)

    @pl.when(col == 0)
    def _():
        headbuf[...] = headbuf[...] - correction

    pl.when(z == 0)(produce)

    @pl.when(row == 0)
    def _():
        pt[:, 0:128] = pt[:, 0:128] - correction

    arrived(0, leaf3.at[0])
    arrived(2, leaf4.at[0])
    low_side = zsum[z_peer(-2)] + leaf3[0]
    relay[0, :, 0:half] = low_side[:, 0:half] + leaf4[0]
    relay[0, :, half:] = low_side[:, half:]
    arrived(1, leaf3.at[1])
    arrived(3, leaf4.at[1])
    high_side = zsum[z_peer(2)] + leaf3[1]
    relay[1, :, 0:half] = high_side[:, 0:half]
    relay[1, :, half:] = high_side[:, half:] + leaf4[1]
    stage_two(lambda copy: copy.start())

    load_f.wait()
    inner = cross(fv[...], pt[:, own_columns])
    for g in range(nz):
        columns = pl.ds(pl.multiple_of((core * nz + g) * chunk, chunk), chunk)
        inner = inner + cross(zsum[g], pt[:, columns])
    h1send[...] = pack(wide(inner))
    h1buf[row] = h1send[...]

    for k in range(1, nrow):
        remote(h1send, h1buf.at[row], h1_ssem, h1_rsem, {"row": row_peer(k)}).start()

    @pl.when(row == 0)
    def _():
        extra = pltpu.make_async_copy(far.at[:, head_columns], obuf, load_sem.at[4])
        extra.start()
        head = sv.shape[1] * ncol
        ph, plow = split(pt[:, 0:head])
        sh, sl = split(sv[0:head, :])
        both = narrow(jnp.concatenate([ph, plow], 0), sh, NN)
        product = both[:nb] + both[nb:] + narrow(ph, sl, NN)
        extra.wait()
        osend[...] = product + obuf[...]
        obuf[...] = osend[...]

        for k in range(1, nrow):
            remote(osend, obuf, o_ssem, o_rsem, {"row": row_peer(k)}).start()

    flipped_inverse = (pltpu.roll(table, 128 - nb, 1) * flip)[:, :nb]
    shifted_t = jnp.where(lanes == rows, 1.0, 0.0) - jnp.where(
        lanes < nb, pltpu.roll(table, 128 - 2 * nb, 1) * flip, 0.0
    )
    shifted = wide(shifted_t[:, :nb].T)
    augment = jnp.where(lanes == rows + nb, 1.0, 0.0)
    lower_table, upper_table = eliminate([shifted + augment, shifted_t + augment], nb)
    diagonal = jnp.sum(jnp.where(lanes == rows, upper_table, 0.0), axis=1, keepdims=True)
    lower_inverse = pltpu.roll(lower_table, 128 - nb, 1)[:, :nb]
    upper_inverse_t = (pltpu.roll(upper_table, 128 - nb, 1) / diagonal)[:, :nb]
    mixing_t = -exact(upper_inverse_t, flipped_inverse)
    second_t = -exact(lower_inverse, flipped_inverse)

    arrived(4, near.at[0])
    arrived(5, near.at[1])
    arrived(6, twos.at[0])
    arrived(7, twos.at[1])
    zown[...] = (fv[...] + zsum[z]) + (near[0] + near[1]) + (twos[0] + twos[1])

    def slot(k):
        return images.at[core * nz + z_peer(k)]

    def half_slot(k, part):
        return images.at[core * nz + z_peer(k), :, pl.ds(part * half, half)]

    def gather(k):
        return remote(zown, slot(0), a_ssem.at[k % 8], a_rsem.at[-k % 8], chip(k))

    def got(k):
        remote(slot(k), slot(k), a_ssem.at[0], a_rsem.at[k % 8], partner).wait_recv()

    def got_half(part):
        remote(half_slot(4, part), half_slot(4, part), a_ssem.at[0], a_rsem.at[4 * part], partner).wait_recv()

    def pass_on():
        return (
            remote(slot(-2), slot(-2), a_ssem.at[3], a_rsem.at[5], chip(1)),
            remote(half_slot(-2, 0), half_slot(-2, 0), a_ssem.at[4], a_rsem.at[0], chip(2)),
            remote(slot(2), slot(2), a_ssem.at[5], a_rsem.at[3], chip(-1)),
            remote(half_slot(2, 1), half_slot(2, 1), a_ssem.at[0], a_rsem.at[4], chip(-2)),
        )

    def share_chunk(src, k):
        return remote(src, slot(k), f_ssem, f_rsem, partner)

    for k in (2, -2, 1, -1):
        gather(k).start()
    keep = pltpu.make_async_copy(zown, slot(0), image_sem)
    keep.start()
    share_chunk(zown, 0).start()
    copies = pass_on()

    others(h1buf, nrow, h1_ssem, h1_rsem).wait_recv()
    share = h1buf[0]
    for r in range(1, nrow):
        share = share + h1buf[r]
    pairsend[...] = share
    pair = remote(pairsend, pairbuf, pair_sem.at[0], pair_sem.at[1], partner)
    pair.start()

    got(-2)
    copies[0].start()
    copies[1].start()
    share_chunk(slot(-2), -2).start()
    got(2)
    copies[2].start()
    copies[3].start()
    share_chunk(slot(2), 2).start()

    pair.wait_recv()
    share = share + pairbuf[...]
    h2send[...] = share
    h2buf[z] = share
    for k in range(1, nz):
        remote(h2send, h2buf.at[z], h2_ssem, h2_rsem, chip(k)).start()

    for k in (1, -1):
        got(k)
        share_chunk(slot(k), k).start()

    own_reflectors = exact(mixing_t, headbuf[...])
    bottom = exact(second_t, own_reflectors, TN)
    kernel_t = exact(second_t, mixing_t, TN)

    @pl.when(row != 0)
    def _():
        remote(obuf, obuf, o_ssem, o_rsem, {"row": 0}).wait_recv()

    own_base = exact(second_t, obuf[...])

    for k in (3, -3):
        got(k)
        share_chunk(slot(k), k).start()
    got_half(0)
    got_half(1)
    share_chunk(slot(4), 4).start()

    others(h2buf, nz, h2_ssem, h2_rsem).wait_recv()

    inner_total = h2buf[0]
    for c in range(1, nz):
        inner_total = inner_total + h2buf[c]
    inner_t = unpack(inner_total, lanes)[:, :nb]
    weight_t = -0.5 * exact(exact(second_t, inner_t), kernel_t)
    own_weights = own_base + exact(weight_t, headbuf[...])
    top_part = exact(mixing_t, own_weights, TN) + exact(weight_t, own_reflectors, TN)
    coefs[0:nb, :] = top_part
    coefs[nb : 2 * nb, :] = bottom
    coefs[2 * nb : 3 * nb, :] = wide(jnp.concatenate([weight_t, second_t], 1))
    coefs[3 * nb :, :] = jnp.where(row == 0, correction, 0.0)

    theirs = images.at[pl.ds((1 - core) * nz, nz)]
    remote(theirs, theirs, f_ssem, f_rsem, partner).wait_recv()

    keep.wait()

    remote(zout, pbuf, p_ssem, p_rsem.at[0], partner).wait_send()
    mine = images.at[pl.ds(0, nz)]
    remote(mine, mine, f_ssem, f_rsem, partner).wait_send()
    leaves(lambda copy: copy.wait_send())
    nears(lambda copy: copy.wait_send())
    stage_two(lambda copy: copy.wait_send())
    for k in (2, -2, 1, -1):
        gather(k).wait_send()
    for copy in copies:
        copy.wait_send()
    others(gbuf, nrow, g_ssem, g_rsem).wait_send()
    others(h1buf, nrow, h1_ssem, h1_rsem).wait_send()
    others(h2buf, nz, h2_ssem, h2_rsem).wait_send()
    pair.wait_send()

    @pl.when(row == 0)
    def _():
        heads = pv.at[:, pl.ds(0, 128 * (nrow - 1))]
        remote(heads, heads, t_ssem, t_rsem, partner).wait_send()
        remote(heads, heads, o_ssem, o_rsem, partner).wait_send()


def update_kernel(groups, slab, panel, images, coefs, updated, factor, uv, wv, out_sem):
    nb = 32
    parts = images.shape[0] // groups
    chunk = images.shape[2]
    length = parts * chunk

    def writes(g):
        span = pl.ds(g * length, length)
        return (
            pltpu.make_async_copy(wv.at[:, span], factor.at[:, span], out_sem.at[0, g]),
            pltpu.make_async_copy(uv.at[span, :], updated.at[span, :], out_sem.at[1, g]),
        )

    bh, bl = split(coefs[0 : 2 * nb, :])
    right = jnp.concatenate([bh, bl, bh], 0)
    ch, cl = split(coefs[2 * nb : 3 * nb, 0 : 2 * nb])
    left = jnp.concatenate([ch, ch, cl], 1)
    for g in range(groups):
        for i in range(g * parts, (g + 1) * parts):
            piece = slice(i * chunk, (i + 1) * chunk)
            columns = panel[:, piece]
            if i == 0:
                columns = jnp.concatenate(
                    [columns[:, 0:128] - coefs[3 * nb :, :], columns[:, 128:]], 1
                )
            xh, xl = split(jnp.concatenate([columns, images[i]], 0))
            wv[:, piece] = narrow(left, jnp.concatenate([xh, xl, xh], 0), NN)
            uv[piece, :] = slab[piece, :] - narrow(jnp.concatenate([xh, xh, xl], 0), right, TN)
        for copy in writes(g):
            copy.start()
    for g in range(groups):
        for copy in writes(g):
            copy.wait()


def local(nrow, ncol, slab, panel, far):
    nb, length = panel.shape
    chunk = length // ncol
    nz = ncol // 2
    anywhere = pl.BlockSpec(memory_space=pl.ANY)
    vmem = pl.BlockSpec(memory_space=pltpu.VMEM)
    dma = pltpu.SemaphoreType.DMA
    strip = pltpu.VMEM((nb, 128), F32)
    tile = pltpu.VMEM((8, 128), F32)

    def chunks(n, width=chunk):
        return pltpu.VMEM((n, nb, width), F32)

    images, coefs = pl.pallas_call(
        functools.partial(exchange_kernel, nrow, ncol),
        name="exchange",
        out_shape=(
            jax.ShapeDtypeStruct((ncol, nb, chunk), F32),
            jax.ShapeDtypeStruct((4 * nb, 128), F32),
        ),
        in_specs=[anywhere] * 3,
        out_specs=(anywhere, vmem),
        scratch_shapes=[
            pltpu.VMEM((nb, length), F32),
            pltpu.VMEM(slab.shape, F32),
            pltpu.VMEM((nb, chunk), F32),
            pltpu.VMEM((16, 128), F32),
            pltpu.VMEM((nrow, 16, 128), F32),
            strip,
            pltpu.VMEM((nb, length), F32),
            chunks(nz), chunks(nz), chunks(nz),
            chunks(2), chunks(2, chunk // 2), chunks(2), chunks(2), chunks(2),
            pltpu.VMEM((nb, chunk), F32),
            strip, strip,
            tile, pltpu.VMEM((nrow, 8, 128), F32),
            tile, pltpu.VMEM((nz, 8, 128), F32),
            tile, tile,
            dma((5,)),
            dma(()), dma(()),
            dma(()), dma(()),
            dma(()), dma((nz,)),
            dma((8,)), dma((8,)),
            dma((8,)), dma((8,)),
            dma(()), dma(()),
            dma(()), dma(()),
            dma(()), dma(()),
            dma(()), dma(()),
            dma((2,)), dma(()),
        ],
        compiler_params=pltpu.CompilerParams(
            collective_id=0, has_side_effects=True, vmem_limit_bytes=24 * 2**20
        ),
    )(*(pltpu.with_memory_space_constraint(array, pltpu.HBM) for array in (slab, panel, far)))
    groups = 4
    return pl.pallas_call(
        functools.partial(update_kernel, groups),
        name="update",
        out_shape=(
            jax.ShapeDtypeStruct(slab.shape, F32),
            jax.ShapeDtypeStruct(panel.shape, F32),
        ),
        in_specs=[vmem] * 4,
        out_specs=(anywhere, anywhere),
        scratch_shapes=[
            pltpu.VMEM(slab.shape, F32),
            pltpu.VMEM(panel.shape, F32),
            dma((2, groups)),
        ],
        compiler_params=pltpu.CompilerParams(vmem_limit_bytes=24 * 2**20),
    )(slab, panel, images, coefs)


def solution(mesh):
    sizes = dict(mesh.shape)
    body = functools.partial(local, sizes["row"], sizes["col"])
    in_specs = (P("row", "col"), P(None, "row"), P(None, "row"))
    out_specs = (P("row", "col"), P(None, "row"))
    return jax.shard_map(body, mesh=mesh, in_specs=in_specs, out_specs=out_specs, check_vma=False)
```

```python
import functools

import jax
import jax.numpy as jnp
from jax import lax
from jax.experimental import pallas as pl
from jax.experimental.pallas import tpu as pltpu
from jax.sharding import PartitionSpec as P

F32 = jnp.float32
BF16 = jnp.bfloat16
MESH = pl.DeviceIdType.MESH
NT = (((1,), (1,)), ((), ()))
TN = (((0,), (0,)), ((), ()))
NN = (((1,), (0,)), ((), ()))


def exact(left, right, dims=NN):
    return lax.dot_general(
        left, right, dims, precision=lax.Precision.HIGHEST, preferred_element_type=F32
    )


def narrow(left, right, dims):
    return lax.dot_general(left, right, dims, preferred_element_type=F32)


def split(x):
    high = x.astype(BF16)
    low = (x - high.astype(F32)).astype(BF16)
    return high, low


def split3(x):
    high = x.astype(BF16)
    rest = x - high.astype(F32)
    mid = rest.astype(BF16)
    low = (rest - mid.astype(F32)).astype(BF16)
    return high, mid, low


def gram_of(block):
    nb = block.shape[0]
    one, two, three = split3(block)
    first = narrow(jnp.concatenate([one, two, three], 0), one, NT)
    second = narrow(jnp.concatenate([one, two], 0), two, NT)
    third = narrow(one, three, NT)
    return (
        first[:nb]
        + (first[nb : 2 * nb] + second[:nb])
        + (first[2 * nb :] + second[nb:] + third)
    )


def cross(left, right):
    nb = left.shape[0]
    lh, ll = split(left)
    rh, rl = split(right)
    both = narrow(jnp.concatenate([lh, ll], 0), rh, NT)
    return both[:nb] + both[nb:] + narrow(lh, rl, NT)


def eliminate(tables, nb):
    rows = lax.broadcasted_iota(jnp.int32, (nb, 128), 0)
    for j in range(0, nb, 2):
        done = []
        for table in tables:
            column = jnp.broadcast_to(table[:, j : j + 1], (nb, 128))
            following = jnp.broadcast_to(table[:, j + 1 : j + 2], (nb, 128))
            pivot = column[j : j + 1, :]
            pivot_row = table[j : j + 1, :] / pivot
            below = jnp.where(rows > j, column, 0.0)
            following = following - below * (following[j : j + 1, :] / pivot)
            next_row = table[j + 1 : j + 2, :] - column[j + 1 : j + 2, :] * pivot_row
            next_row = next_row / following[j + 1 : j + 2, :]
            after = jnp.where(rows > j + 1, following, 0.0)
            done.append(table - below * pivot_row - after * next_row)
        tables = done
    return tables


def pack(square):
    total = square[0:8]
    for k in range(1, 4):
        total = total + pltpu.roll(square[8 * k : 8 * k + 8], 32 * k, 1)
    return total


def unpack(packed, lanes):
    parts = [packed] + [pltpu.roll(packed, 128 - 32 * k, 1) for k in range(1, 4)]
    return jnp.where(lanes < 32, jnp.concatenate(parts, 0), 0.0)


def wide(square):
    return jnp.concatenate([square, jnp.zeros((square.shape[0], 128 - square.shape[1]), F32)], 1)


def exchange_kernel(
    nrow, ncol,
    slab, panel, far,
    images, coefs,
    pv, sv, fv, gsend, gbuf, headbuf, pt, zout, pbuf, zsum,
    leaf3, leaf4, near, relay, twos, zown, osend, obuf, h1send, h1buf, h2send, h2buf, pairsend, pairbuf,
    load_sem, g_ssem, g_rsem, t_ssem, t_rsem, p_ssem, p_rsem, r_ssem, r_rsem,
    a_ssem, a_rsem, f_ssem, f_rsem, o_ssem, o_rsem, h1_ssem, h1_rsem, h2_ssem, h2_rsem,
    pair_sem, image_sem,
):
    nb = 32
    nz = ncol // 2
    chunk = pv.shape[1] // ncol
    half = chunk // 2
    row = lax.axis_index("row")
    col = lax.axis_index("col")
    z = lax.div(col, 2)
    core = lax.rem(col, 2)
    partner = {"col": col + 1 - 2 * core}
    rows = lax.broadcasted_iota(jnp.int32, (nb, 128), 0)
    lanes = lax.broadcasted_iota(jnp.int32, (nb, 128), 1)

    def remote(src, dst, ssem, rsem, device):
        return pltpu.make_async_remote_copy(
            src_ref=src, dst_ref=dst, send_sem=ssem, recv_sem=rsem,
            device_id=device, device_id_type=MESH,
        )

    def others(buffer, n, ssem, rsem):
        slots = buffer.at[pl.ds(0, n - 1)]
        return remote(slots, slots, ssem, rsem, partner)

    def row_peer(k):
        return lax.rem(row + k, nrow)

    def z_peer(k):
        return lax.rem(z + k + nz, nz)

    def chip(k):
        return {"col": 2 * z_peer(k) + core}

    load_p = pltpu.make_async_copy(panel, pv, load_sem.at[0])
    load_s = pltpu.make_async_copy(slab, sv, load_sem.at[1])
    own = core * nz + z
    own_columns = pl.ds(pl.multiple_of(own * chunk, chunk), chunk)
    load_f = pltpu.make_async_copy(far.at[:, own_columns], fv, load_sem.at[2])
    load_p.start()
    load_s.start()
    load_f.start()

    barrier = pltpu.get_barrier_semaphore()

    @pl.loop(1, nrow)
    def _(k):
        pl.semaphore_signal(barrier, inc=1, device_id={"row": row_peer(k)}, device_id_type=MESH)

    for device in (partner, chip(1), chip(-1), chip(2), chip(-2)):
        pl.semaphore_signal(barrier, inc=1, device_id=device, device_id_type=MESH)

    load_p.wait()
    gram = jnp.zeros((nb, nb), F32)
    for g in range(ncol):
        gram = gram + gram_of(pv[:, g * chunk : (g + 1) * chunk])
    gsend[0:8, :] = pack(wide(gram))
    gsend[8:16, :] = pack(jnp.where(lanes < nb, pv[:, 0:128], 0.0))
    gbuf[row] = gsend[...]
    pt[...] = pv[...]
    pl.semaphore_wait(barrier, nrow + 4)

    head_columns = pl.ds(pl.multiple_of(col * 128, 128), 128)

    for k in range(1, nrow):
        remote(gsend, gbuf.at[row], g_ssem, g_rsem, {"row": row_peer(k)}).start()

    @pl.when(row == 0)
    def _():
        for k in range(1, nrow):
            remote(pv.at[:, head_columns], headbuf, t_ssem, t_rsem, {"row": row_peer(k)}).start()
        local_head = pltpu.make_async_copy(pv.at[:, head_columns], headbuf, load_sem.at[3])
        local_head.start()
        local_head.wait()

    load_s.wait()

    @pl.when(row != 0)
    def _():
        remote(headbuf, headbuf, t_ssem, t_rsem, {"row": 0}).wait_recv()

    def produce():
        high, low = split(headbuf[...])
        weights = jnp.concatenate(
            [
                jnp.concatenate([high, high], 1),
                jnp.concatenate([low, jnp.zeros_like(low)], 1),
            ],
            0,
        )

        def product(index):
            block = sv[pl.ds(pl.multiple_of(index * chunk, chunk), chunk), :]
            sh, sl = split(block)
            both = narrow(weights, jnp.concatenate([sh, sl], 1), NT)
            return both[:nb] + both[nb:]

        def to_partner(peer):
            return remote(zout.at[peer], pbuf.at[peer], p_ssem, p_rsem.at[peer], partner)

        def other_half(k):
            peer = z_peer(k)
            zout[peer] = product((1 - core) * nz + peer)
            to_partner(peer).start()

        def own_half(k):
            peer = z_peer(k)
            part = product(core * nz + peer)
            to_partner(peer).wait_recv()
            zsum[peer] = part + pbuf[peer]

        pl.loop(3, nz)(other_half)
        pl.loop(3, nz - 2)(own_half)
        leaves(lambda copy: copy.start())
        pl.loop(nz, nz + 3)(other_half)
        pl.loop(nz - 2, nz + 3)(own_half)
        nears(lambda copy: copy.start())

    def leaves(act):
        act(remote(zsum.at[z_peer(-3)], leaf3.at[0], r_ssem.at[0], r_rsem.at[0], chip(-1)))
        act(remote(zsum.at[z_peer(3)], leaf3.at[1], r_ssem.at[1], r_rsem.at[1], chip(1)))
        first = zsum.at[z_peer(4), :, pl.ds(0, half)]
        second = zsum.at[z_peer(4), :, pl.ds(half, half)]
        act(remote(first, leaf4.at[0], r_ssem.at[2], r_rsem.at[2], chip(-2)))
        act(remote(second, leaf4.at[1], r_ssem.at[3], r_rsem.at[3], chip(2)))

    def nears(act):
        act(remote(zsum.at[z_peer(-1)], near.at[0], r_ssem.at[4], r_rsem.at[4], chip(-1)))
        act(remote(zsum.at[z_peer(1)], near.at[1], r_ssem.at[5], r_rsem.at[5], chip(1)))

    stage_two = (
        remote(relay.at[0], twos.at[0], r_ssem.at[6], r_rsem.at[6], chip(-2)),
        remote(relay.at[1], twos.at[1], r_ssem.at[7], r_rsem.at[7], chip(2)),
    )

    def arrived(index, slot):
        remote(slot, slot, r_ssem.at[index], r_rsem.at[index], partner).wait_recv()

    pl.when(z != 0)(produce)

    others(gbuf, nrow, g_ssem, g_rsem).wait_recv()

    total = gbuf[0, 0:8]
    for r in range(1, nrow):
        total = total + gbuf[r, 0:8]
    table = (
        unpack(total, lanes)
        + jnp.where(lanes == rows + nb, 1.0, 0.0)
        + pltpu.roll(unpack(gbuf[0, 8:16], lanes), 2 * nb, 1)
    )
    (table,) = eliminate([table], nb)
    pivots = jnp.sum(jnp.where(lanes == rows, table, 0.0), axis=1, keepdims=True)
    table = table / jnp.sqrt(pivots)
    signs = jnp.sum(jnp.where(lanes == rows + 2 * nb, table, 0.0), axis=1, keepdims=True)
    flip = jnp.where(signs >= 0.0, -1.0, 1.0).astype(F32)
    upper = jnp.where((lanes >= rows) & (lanes < nb), table * flip, 0.0)
    correction = wide(upper[:, :nb].T)

    @pl.when(col == 0)
    def _():
        headbuf[...] = headbuf[...] - correction

    pl.when(z == 0)(produce)

    @pl.when(row == 0)
    def _():
        pt[:, 0:128] = pt[:, 0:128] - correction

    arrived(0, leaf3.at[0])
    arrived(2, leaf4.at[0])
    low_side = zsum[z_peer(-2)] + leaf3[0]
    relay[0, :, 0:half] = low_side[:, 0:half] + leaf4[0]
    relay[0, :, half:] = low_side[:, half:]
    stage_two[0].start()
    arrived(1, leaf3.at[1])
    arrived(3, leaf4.at[1])
    high_side = zsum[z_peer(2)] + leaf3[1]
    relay[1, :, 0:half] = high_side[:, 0:half]
    relay[1, :, half:] = high_side[:, half:] + leaf4[1]
    stage_two[1].start()

    load_f.wait()
    inner = cross(fv[...], pt[:, own_columns])
    for g in range(nz):
        columns = pl.ds(pl.multiple_of((core * nz + g) * chunk, chunk), chunk)
        inner = inner + cross(zsum[g], pt[:, columns])
    h1send[...] = pack(wide(inner))
    h1buf[row] = h1send[...]

    for k in range(1, nrow):
        remote(h1send, h1buf.at[row], h1_ssem, h1_rsem, {"row": row_peer(k)}).start()

    @pl.when(row == 0)
    def _():
        extra = pltpu.make_async_copy(far.at[:, head_columns], obuf, load_sem.at[4])
        extra.start()
        head = sv.shape[1] * ncol
        ph, plow = split(pt[:, 0:head])
        sh, sl = split(sv[0:head, :])
        both = narrow(jnp.concatenate([ph, plow], 0), sh, NN)
        product = both[:nb] + both[nb:] + narrow(ph, sl, NN)
        extra.wait()
        osend[...] = product + obuf[...]
        obuf[...] = osend[...]

        for k in range(1, nrow):
            remote(osend, obuf, o_ssem, o_rsem, {"row": row_peer(k)}).start()

    flipped_inverse = (pltpu.roll(table, 128 - nb, 1) * flip)[:, :nb]
    shifted_t = jnp.where(lanes == rows, 1.0, 0.0) - jnp.where(
        lanes < nb, pltpu.roll(table, 128 - 2 * nb, 1) * flip, 0.0
    )
    shifted = wide(shifted_t[:, :nb].T)
    augment = jnp.where(lanes == rows + nb, 1.0, 0.0)
    lower_table, upper_table = eliminate([shifted + augment, shifted_t + augment], nb)
    diagonal = jnp.sum(jnp.where(lanes == rows, upper_table, 0.0), axis=1, keepdims=True)
    lower_inverse = pltpu.roll(lower_table, 128 - nb, 1)[:, :nb]
    upper_inverse_t = (pltpu.roll(upper_table, 128 - nb, 1) / diagonal)[:, :nb]
    mixing_t = -exact(upper_inverse_t, flipped_inverse)
    second_t = -exact(lower_inverse, flipped_inverse)

    arrived(4, near.at[0])
    arrived(5, near.at[1])
    arrived(6, twos.at[0])
    arrived(7, twos.at[1])
    zown[...] = (fv[...] + zsum[z]) + (near[0] + near[1]) + (twos[0] + twos[1])

    def slot(k):
        return images.at[core * nz + z_peer(k)]

    def half_slot(k, part):
        return images.at[core * nz + z_peer(k), :, pl.ds(part * half, half)]

    def half_own(part):
        return zown.at[:, pl.ds(part * half, half)]

    def got(ref, n):
        remote(ref, ref, a_ssem.at[0], a_rsem.at[n], partner).wait_recv()

    def onward(k, part, n, m, device):
        piece = half_slot(k, part)
        return remote(piece, piece, a_ssem.at[n], a_rsem.at[m], device)

    gather = (
        remote(half_own(0), half_slot(0, 0), a_ssem.at[0], a_rsem.at[0], chip(2)),
        remote(half_own(1), half_slot(0, 1), a_ssem.at[1], a_rsem.at[3], chip(-2)),
        remote(half_own(1), half_slot(0, 1), a_ssem.at[2], a_rsem.at[1], chip(2)),
        remote(half_own(0), half_slot(0, 0), a_ssem.at[3], a_rsem.at[2], chip(-2)),
        remote(zown, slot(0), a_ssem.at[4], a_rsem.at[4], chip(1)),
        remote(zown, slot(0), a_ssem.at[5], a_rsem.at[5], chip(-1)),
    )
    copies = (
        onward(-2, 0, 6, 10, chip(2)),
        onward(-2, 0, 7, 6, chip(1)),
        onward(2, 1, 8, 11, chip(-2)),
        onward(2, 1, 9, 9, chip(-1)),
        onward(-2, 1, 10, 7, chip(1)),
        onward(2, 0, 11, 8, chip(-1)),
    )

    def share_chunk(src, k):
        return remote(src, slot(k), f_ssem, f_rsem, partner)

    for copy in gather:
        copy.start()
    keep = pltpu.make_async_copy(zown, slot(0), image_sem)
    keep.start()
    share_chunk(zown, 0).start()
    others(h1buf, nrow, h1_ssem, h1_rsem).wait_recv()
    share = h1buf[0]
    for r in range(1, nrow):
        share = share + h1buf[r]
    pairsend[...] = share
    pair = remote(pairsend, pairbuf, pair_sem.at[0], pair_sem.at[1], partner)
    pair.start()

    got(half_slot(-2, 0), 0)
    copies[0].start()
    copies[1].start()
    got(half_slot(2, 1), 3)
    copies[2].start()
    copies[3].start()
    got(half_slot(-2, 1), 1)
    copies[4].start()
    got(half_slot(2, 0), 2)
    copies[5].start()
    share_chunk(slot(-2), -2).start()
    share_chunk(slot(2), 2).start()

    pair.wait_recv()
    share = share + pairbuf[...]
    h2send[...] = share
    h2buf[z] = share
    for k in range(1, nz):
        remote(h2send, h2buf.at[z], h2_ssem, h2_rsem, chip(k)).start()

    for k, n in ((-1, 4), (1, 5)):
        got(slot(k), n)
        share_chunk(slot(k), k).start()

    own_reflectors = exact(mixing_t, headbuf[...])
    bottom = exact(second_t, own_reflectors, TN)
    kernel_t = exact(second_t, mixing_t, TN)

    @pl.when(row != 0)
    def _():
        remote(obuf, obuf, o_ssem, o_rsem, {"row": 0}).wait_recv()

    own_base = exact(second_t, obuf[...])

    got(half_slot(4, 0), 10)
    got(half_slot(4, 1), 11)
    share_chunk(slot(4), 4).start()
    for k, n in ((-3, 6), (3, 8)):
        got(half_slot(k, 0), n)
        got(half_slot(k, 1), n + 1)
        share_chunk(slot(k), k).start()

    others(h2buf, nz, h2_ssem, h2_rsem).wait_recv()

    inner_total = h2buf[0]
    for c in range(1, nz):
        inner_total = inner_total + h2buf[c]
    inner_t = unpack(inner_total, lanes)[:, :nb]
    weight_t = -0.5 * exact(exact(second_t, inner_t), kernel_t)
    own_weights = own_base + exact(weight_t, headbuf[...])
    top_part = exact(mixing_t, own_weights, TN) + exact(weight_t, own_reflectors, TN)
    coefs[0:nb, :] = top_part
    coefs[nb : 2 * nb, :] = bottom
    coefs[2 * nb : 3 * nb, :] = wide(jnp.concatenate([weight_t, second_t], 1))
    coefs[3 * nb :, :] = jnp.where(row == 0, correction, 0.0)

    theirs = images.at[pl.ds((1 - core) * nz, nz)]
    remote(theirs, theirs, f_ssem, f_rsem, partner).wait_recv()

    keep.wait()

    remote(zout, pbuf, p_ssem, p_rsem.at[0], partner).wait_send()
    mine = images.at[pl.ds(0, nz)]
    remote(mine, mine, f_ssem, f_rsem, partner).wait_send()
    leaves(lambda copy: copy.wait_send())
    nears(lambda copy: copy.wait_send())
    for copy in stage_two:
        copy.wait_send()
    for copy in gather + copies:
        copy.wait_send()
    others(gbuf, nrow, g_ssem, g_rsem).wait_send()
    others(h1buf, nrow, h1_ssem, h1_rsem).wait_send()
    others(h2buf, nz, h2_ssem, h2_rsem).wait_send()
    pair.wait_send()

    @pl.when(row == 0)
    def _():
        heads = pv.at[:, pl.ds(0, 128 * (nrow - 1))]
        remote(heads, heads, t_ssem, t_rsem, partner).wait_send()
        remote(heads, heads, o_ssem, o_rsem, partner).wait_send()


def update_kernel(groups, slab, panel, images, coefs, updated, factor, uv, wv, out_sem):
    nb = 32
    parts = images.shape[0] // groups
    chunk = images.shape[2]
    length = parts * chunk

    def writes(g):
        span = pl.ds(g * length, length)
        return (
            pltpu.make_async_copy(wv.at[:, span], factor.at[:, span], out_sem.at[0, g]),
            pltpu.make_async_copy(uv.at[span, :], updated.at[span, :], out_sem.at[1, g]),
        )

    bh, bl = split(coefs[0 : 2 * nb, :])
    right = jnp.concatenate([bh, bl, bh], 0)
    ch, cl = split(coefs[2 * nb : 3 * nb, 0 : 2 * nb])
    left = jnp.concatenate([ch, ch, cl], 1)
    for g in range(groups):
        for i in range(g * parts, (g + 1) * parts):
            piece = slice(i * chunk, (i + 1) * chunk)
            columns = panel[:, piece]
            if i == 0:
                columns = jnp.concatenate(
                    [columns[:, 0:128] - coefs[3 * nb :, :], columns[:, 128:]], 1
                )
            xh, xl = split(jnp.concatenate([columns, images[i]], 0))
            wv[:, piece] = narrow(left, jnp.concatenate([xh, xl, xh], 0), NN)
            uv[piece, :] = slab[piece, :] - narrow(jnp.concatenate([xh, xh, xl], 0), right, TN)
        for copy in writes(g):
            copy.start()
    for g in range(groups):
        for copy in writes(g):
            copy.wait()


def local(nrow, ncol, slab, panel, far):
    nb, length = panel.shape
    chunk = length // ncol
    nz = ncol // 2
    anywhere = pl.BlockSpec(memory_space=pl.ANY)
    vmem = pl.BlockSpec(memory_space=pltpu.VMEM)
    dma = pltpu.SemaphoreType.DMA
    strip = pltpu.VMEM((nb, 128), F32)
    tile = pltpu.VMEM((8, 128), F32)

    def chunks(n, width=chunk):
        return pltpu.VMEM((n, nb, width), F32)

    images, coefs = pl.pallas_call(
        functools.partial(exchange_kernel, nrow, ncol),
        name="exchange",
        out_shape=(
            jax.ShapeDtypeStruct((ncol, nb, chunk), F32),
            jax.ShapeDtypeStruct((4 * nb, 128), F32),
        ),
        in_specs=[anywhere] * 3,
        out_specs=(anywhere, vmem),
        scratch_shapes=[
            pltpu.VMEM((nb, length), F32),
            pltpu.VMEM(slab.shape, F32),
            pltpu.VMEM((nb, chunk), F32),
            pltpu.VMEM((16, 128), F32),
            pltpu.VMEM((nrow, 16, 128), F32),
            strip,
            pltpu.VMEM((nb, length), F32),
            chunks(nz), chunks(nz), chunks(nz),
            chunks(2), chunks(2, chunk // 2), chunks(2), chunks(2), chunks(2),
            pltpu.VMEM((nb, chunk), F32),
            strip, strip,
            tile, pltpu.VMEM((nrow, 8, 128), F32),
            tile, pltpu.VMEM((nz, 8, 128), F32),
            tile, tile,
            dma((5,)),
            dma(()), dma(()),
            dma(()), dma(()),
            dma(()), dma((nz,)),
            dma((8,)), dma((8,)),
            dma((12,)), dma((12,)),
            dma(()), dma(()),
            dma(()), dma(()),
            dma(()), dma(()),
            dma(()), dma(()),
            dma((2,)), dma(()),
        ],
        compiler_params=pltpu.CompilerParams(
            collective_id=0, has_side_effects=True, vmem_limit_bytes=24 * 2**20
        ),
    )(*(pltpu.with_memory_space_constraint(array, pltpu.HBM) for array in (slab, panel, far)))
    groups = 4
    return pl.pallas_call(
        functools.partial(update_kernel, groups),
        name="update",
        out_shape=(
            jax.ShapeDtypeStruct(slab.shape, F32),
            jax.ShapeDtypeStruct(panel.shape, F32),
        ),
        in_specs=[vmem] * 4,
        out_specs=(anywhere, anywhere),
        scratch_shapes=[
            pltpu.VMEM(slab.shape, F32),
            pltpu.VMEM(panel.shape, F32),
            dma((2, groups)),
        ],
        compiler_params=pltpu.CompilerParams(vmem_limit_bytes=24 * 2**20),
    )(slab, panel, images, coefs)


def solution(mesh):
    sizes = dict(mesh.shape)
    body = functools.partial(local, sizes["row"], sizes["col"])
    in_specs = (P("row", "col"), P(None, "row"), P(None, "row"))
    out_specs = (P("row", "col"), P(None, "row"))
    return jax.shard_map(body, mesh=mesh, in_specs=in_specs, out_specs=out_specs, check_vma=False)
```

```python
import functools

import jax
import jax.numpy as jnp
from jax import lax
from jax.experimental import pallas as pl
from jax.experimental.pallas import tpu as pltpu
from jax.sharding import PartitionSpec as P

F32 = jnp.float32
BF16 = jnp.bfloat16
MESH = pl.DeviceIdType.MESH
NT = (((1,), (1,)), ((), ()))
TN = (((0,), (0,)), ((), ()))
NN = (((1,), (0,)), ((), ()))


def exact(left, right, dims=NN):
    return lax.dot_general(
        left, right, dims, precision=lax.Precision.HIGHEST, preferred_element_type=F32
    )


def narrow(left, right, dims):
    return lax.dot_general(left, right, dims, preferred_element_type=F32)


def split(x):
    high = x.astype(BF16)
    low = (x - high.astype(F32)).astype(BF16)
    return high, low


def split3(x):
    high = x.astype(BF16)
    rest = x - high.astype(F32)
    mid = rest.astype(BF16)
    low = (rest - mid.astype(F32)).astype(BF16)
    return high, mid, low


def gram_of(block):
    nb = block.shape[0]
    one, two, three = split3(block)
    first = narrow(jnp.concatenate([one, two, three], 0), one, NT)
    second = narrow(jnp.concatenate([one, two], 0), two, NT)
    third = narrow(one, three, NT)
    return (
        first[:nb]
        + (first[nb : 2 * nb] + second[:nb])
        + (first[2 * nb :] + second[nb:] + third)
    )


def cross(left, right):
    nb = left.shape[0]
    lh, ll = split(left)
    rh, rl = split(right)
    both = narrow(jnp.concatenate([lh, ll], 0), rh, NT)
    return both[:nb] + both[nb:] + narrow(lh, rl, NT)


def eliminate(tables, nb):
    rows = lax.broadcasted_iota(jnp.int32, (nb, 128), 0)
    for j in range(0, nb, 2):
        done = []
        for table in tables:
            column = jnp.broadcast_to(table[:, j : j + 1], (nb, 128))
            following = jnp.broadcast_to(table[:, j + 1 : j + 2], (nb, 128))
            pivot = column[j : j + 1, :]
            pivot_row = table[j : j + 1, :] / pivot
            below = jnp.where(rows > j, column, 0.0)
            following = following - below * (following[j : j + 1, :] / pivot)
            next_row = table[j + 1 : j + 2, :] - column[j + 1 : j + 2, :] * pivot_row
            next_row = next_row / following[j + 1 : j + 2, :]
            after = jnp.where(rows > j + 1, following, 0.0)
            done.append(table - below * pivot_row - after * next_row)
        tables = done
    return tables


def pack(square):
    total = square[0:8]
    for k in range(1, 4):
        total = total + pltpu.roll(square[8 * k : 8 * k + 8], 32 * k, 1)
    return total


def unpack(packed, lanes):
    parts = [packed] + [pltpu.roll(packed, 128 - 32 * k, 1) for k in range(1, 4)]
    return jnp.where(lanes < 32, jnp.concatenate(parts, 0), 0.0)


def wide(square):
    return jnp.concatenate([square, jnp.zeros((square.shape[0], 128 - square.shape[1]), F32)], 1)


def exchange_kernel(
    nrow, ncol,
    slab, panel, far,
    images, coefs,
    pv, sv, fv, gsend, gbuf, headbuf, pt, zout, pbuf, zsum,
    leaf3, leaf4, near, relay, twos, zown, osend, obuf, h1send, h1buf, h2send, h2buf, pairsend, pairbuf,
    load_sem, g_ssem, g_rsem, t_ssem, t_rsem, p_ssem, p_rsem, r_ssem, r_rsem,
    a_ssem, a_rsem, f_ssem, f_rsem, o_ssem, o_rsem, h1_ssem, h1_rsem, h2_ssem, h2_rsem,
    pair_sem, image_sem,
):
    nb = 32
    nz = ncol // 2
    chunk = pv.shape[1] // ncol
    half = chunk // 2
    row = lax.axis_index("row")
    col = lax.axis_index("col")
    z = lax.div(col, 2)
    core = lax.rem(col, 2)
    partner = {"col": col + 1 - 2 * core}
    rows = lax.broadcasted_iota(jnp.int32, (nb, 128), 0)
    lanes = lax.broadcasted_iota(jnp.int32, (nb, 128), 1)

    def remote(src, dst, ssem, rsem, device):
        return pltpu.make_async_remote_copy(
            src_ref=src, dst_ref=dst, send_sem=ssem, recv_sem=rsem,
            device_id=device, device_id_type=MESH,
        )

    def others(buffer, n, ssem, rsem):
        slots = buffer.at[pl.ds(0, n - 1)]
        return remote(slots, slots, ssem, rsem, partner)

    def row_peer(k):
        return lax.rem(row + k, nrow)

    def z_peer(k):
        return lax.rem(z + k + nz, nz)

    def chip(k):
        return {"col": 2 * z_peer(k) + core}

    load_p = pltpu.make_async_copy(panel, pv, load_sem.at[0])
    load_s = pltpu.make_async_copy(slab, sv, load_sem.at[1])
    own = core * nz + z
    own_columns = pl.ds(pl.multiple_of(own * chunk, chunk), chunk)
    load_f = pltpu.make_async_copy(far.at[:, own_columns], fv, load_sem.at[2])
    load_p.start()
    load_s.start()
    load_f.start()

    barrier = pltpu.get_barrier_semaphore()

    @pl.loop(1, nrow)
    def _(k):
        pl.semaphore_signal(barrier, inc=1, device_id={"row": row_peer(k)}, device_id_type=MESH)

    for device in (partner, chip(1), chip(-1), chip(2), chip(-2)):
        pl.semaphore_signal(barrier, inc=1, device_id=device, device_id_type=MESH)

    load_p.wait()
    gram = jnp.zeros((nb, nb), F32)
    for g in range(ncol):
        gram = gram + gram_of(pv[:, g * chunk : (g + 1) * chunk])
    gsend[0:8, :] = pack(wide(gram))
    gsend[8:16, :] = pack(jnp.where(lanes < nb, pv[:, 0:128], 0.0))
    gbuf[row] = gsend[...]
    pt[...] = pv[...]
    pl.semaphore_wait(barrier, nrow + 4)

    head_columns = pl.ds(pl.multiple_of(col * 128, 128), 128)

    @pl.when(row == 0)
    def _():
        for k in range(1, nrow):
            remote(pv.at[:, head_columns], headbuf, t_ssem, t_rsem, {"row": row_peer(k)}).start()

    for k in range(1, nrow):
        remote(gsend, gbuf.at[row], g_ssem, g_rsem, {"row": row_peer(k)}).start()

    @pl.when(row == 0)
    def _():
        local_head = pltpu.make_async_copy(pv.at[:, head_columns], headbuf, load_sem.at[3])
        local_head.start()
        local_head.wait()

    load_s.wait()

    @pl.when(row != 0)
    def _():
        remote(headbuf, headbuf, t_ssem, t_rsem, {"row": 0}).wait_recv()

    def produce():
        high, low = split(headbuf[...])
        weights = jnp.concatenate(
            [
                jnp.concatenate([high, high], 1),
                jnp.concatenate([low, jnp.zeros_like(low)], 1),
            ],
            0,
        )

        def product(index):
            block = sv[pl.ds(pl.multiple_of(index * chunk, chunk), chunk), :]
            sh, sl = split(block)
            both = narrow(weights, jnp.concatenate([sh, sl], 1), NT)
            return both[:nb] + both[nb:]

        def to_partner(peer):
            return remote(zout.at[peer], pbuf.at[peer], p_ssem, p_rsem.at[peer], partner)

        def other_half(k):
            peer = z_peer(k)
            zout[peer] = product((1 - core) * nz + peer)
            to_partner(peer).start()

        def own_half(k):
            peer = z_peer(k)
            part = product(core * nz + peer)
            to_partner(peer).wait_recv()
            zsum[peer] = part + pbuf[peer]

        pl.loop(3, nz)(other_half)
        pl.loop(3, nz - 2)(own_half)
        leaves(lambda copy: copy.start())
        pl.loop(nz, nz + 3)(other_half)
        pl.loop(nz - 2, nz + 3)(own_half)
        nears(lambda copy: copy.start())

    def leaves(act):
        act(remote(zsum.at[z_peer(-3)], leaf3.at[0], r_ssem.at[0], r_rsem.at[0], chip(-1)))
        act(remote(zsum.at[z_peer(3)], leaf3.at[1], r_ssem.at[1], r_rsem.at[1], chip(1)))
        first = zsum.at[z_peer(4), :, pl.ds(0, half)]
        second = zsum.at[z_peer(4), :, pl.ds(half, half)]
        act(remote(first, leaf4.at[0], r_ssem.at[2], r_rsem.at[2], chip(-2)))
        act(remote(second, leaf4.at[1], r_ssem.at[3], r_rsem.at[3], chip(2)))

    def nears(act):
        act(remote(zsum.at[z_peer(-1)], near.at[0], r_ssem.at[4], r_rsem.at[4], chip(-1)))
        act(remote(zsum.at[z_peer(1)], near.at[1], r_ssem.at[5], r_rsem.at[5], chip(1)))

    stage_two = (
        remote(relay.at[0], twos.at[0], r_ssem.at[6], r_rsem.at[6], chip(-2)),
        remote(relay.at[1], twos.at[1], r_ssem.at[7], r_rsem.at[7], chip(2)),
    )

    def arrived(index, slot):
        remote(slot, slot, r_ssem.at[index], r_rsem.at[index], partner).wait_recv()

    pl.when(z != 0)(produce)

    others(gbuf, nrow, g_ssem, g_rsem).wait_recv()

    total = gbuf[0, 0:8]
    for r in range(1, nrow):
        total = total + gbuf[r, 0:8]
    table = (
        unpack(total, lanes)
        + jnp.where(lanes == rows + nb, 1.0, 0.0)
        + pltpu.roll(unpack(gbuf[0, 8:16], lanes), 2 * nb, 1)
    )
    (table,) = eliminate([table], nb)
    pivots = jnp.sum(jnp.where(lanes == rows, table, 0.0), axis=1, keepdims=True)
    table = table / jnp.sqrt(pivots)
    signs = jnp.sum(jnp.where(lanes == rows + 2 * nb, table, 0.0), axis=1, keepdims=True)
    flip = jnp.where(signs >= 0.0, -1.0, 1.0).astype(F32)
    upper = jnp.where((lanes >= rows) & (lanes < nb), table * flip, 0.0)
    correction = wide(upper[:, :nb].T)

    @pl.when(col == 0)
    def _():
        headbuf[...] = headbuf[...] - correction

    pl.when(z == 0)(produce)

    @pl.when(row == 0)
    def _():
        pt[:, 0:128] = pt[:, 0:128] - correction

    arrived(0, leaf3.at[0])
    arrived(2, leaf4.at[0])
    low_side = zsum[z_peer(-2)] + leaf3[0]
    relay[0, :, 0:half] = low_side[:, 0:half] + leaf4[0]
    relay[0, :, half:] = low_side[:, half:]
    stage_two[0].start()
    arrived(1, leaf3.at[1])
    arrived(3, leaf4.at[1])
    high_side = zsum[z_peer(2)] + leaf3[1]
    relay[1, :, 0:half] = high_side[:, 0:half]
    relay[1, :, half:] = high_side[:, half:] + leaf4[1]
    stage_two[1].start()

    load_f.wait()
    inner = cross(fv[...], pt[:, own_columns])
    for g in range(nz):
        columns = pl.ds(pl.multiple_of((core * nz + g) * chunk, chunk), chunk)
        inner = inner + cross(zsum[g], pt[:, columns])
    h1send[...] = pack(wide(inner))
    h1buf[row] = h1send[...]

    for k in range(1, nrow):
        remote(h1send, h1buf.at[row], h1_ssem, h1_rsem, {"row": row_peer(k)}).start()

    @pl.when(row == 0)
    def _():
        extra = pltpu.make_async_copy(far.at[:, head_columns], obuf, load_sem.at[4])
        extra.start()
        head = sv.shape[1] * ncol
        ph, plow = split(pt[:, 0:head])
        sh, sl = split(sv[0:head, :])
        both = narrow(jnp.concatenate([ph, plow], 0), sh, NN)
        product = both[:nb] + both[nb:] + narrow(ph, sl, NN)
        extra.wait()
        osend[...] = product + obuf[...]
        obuf[...] = osend[...]

        for k in range(1, nrow):
            remote(osend, obuf, o_ssem, o_rsem, {"row": row_peer(k)}).start()

    flipped_inverse = (pltpu.roll(table, 128 - nb, 1) * flip)[:, :nb]
    shifted_t = jnp.where(lanes == rows, 1.0, 0.0) - jnp.where(
        lanes < nb, pltpu.roll(table, 128 - 2 * nb, 1) * flip, 0.0
    )
    shifted = wide(shifted_t[:, :nb].T)
    augment = jnp.where(lanes == rows + nb, 1.0, 0.0)
    lower_table, upper_table = eliminate([shifted + augment, shifted_t + augment], nb)
    diagonal = jnp.sum(jnp.where(lanes == rows, upper_table, 0.0), axis=1, keepdims=True)
    lower_inverse = pltpu.roll(lower_table, 128 - nb, 1)[:, :nb]
    upper_inverse_t = (pltpu.roll(upper_table, 128 - nb, 1) / diagonal)[:, :nb]
    mixing_t = -exact(upper_inverse_t, flipped_inverse)
    second_t = -exact(lower_inverse, flipped_inverse)

    arrived(4, near.at[0])
    arrived(5, near.at[1])
    arrived(6, twos.at[0])
    arrived(7, twos.at[1])
    zown[...] = (fv[...] + zsum[z]) + (near[0] + near[1]) + (twos[0] + twos[1])

    def slot(k):
        return images.at[core * nz + z_peer(k)]

    def half_slot(k, part):
        return images.at[core * nz + z_peer(k), :, pl.ds(part * half, half)]

    def half_own(part):
        return zown.at[:, pl.ds(part * half, half)]

    def got(ref, n):
        remote(ref, ref, a_ssem.at[0], a_rsem.at[n], partner).wait_recv()

    def onward(k, part, n, m, device):
        piece = half_slot(k, part)
        return remote(piece, piece, a_ssem.at[n], a_rsem.at[m], device)

    gather = (
        remote(half_own(0), half_slot(0, 0), a_ssem.at[0], a_rsem.at[0], chip(2)),
        remote(half_own(1), half_slot(0, 1), a_ssem.at[1], a_rsem.at[3], chip(-2)),
        remote(half_own(1), half_slot(0, 1), a_ssem.at[2], a_rsem.at[1], chip(2)),
        remote(half_own(0), half_slot(0, 0), a_ssem.at[3], a_rsem.at[2], chip(-2)),
        remote(zown, slot(0), a_ssem.at[4], a_rsem.at[4], chip(1)),
        remote(zown, slot(0), a_ssem.at[5], a_rsem.at[5], chip(-1)),
    )
    copies = (
        onward(-2, 0, 6, 10, chip(2)),
        onward(-2, 0, 7, 6, chip(1)),
        onward(2, 1, 8, 11, chip(-2)),
        onward(2, 1, 9, 9, chip(-1)),
        onward(-2, 1, 10, 7, chip(1)),
        onward(2, 0, 11, 8, chip(-1)),
    )

    def share_chunk(src, k):
        return remote(src, slot(k), f_ssem, f_rsem, partner)

    for copy in gather:
        copy.start()
    keep = pltpu.make_async_copy(zown, slot(0), image_sem)
    keep.start()
    share_chunk(zown, 0).start()
    others(h1buf, nrow, h1_ssem, h1_rsem).wait_recv()
    share = h1buf[0]
    for r in range(1, nrow):
        share = share + h1buf[r]
    pairsend[...] = share
    pair = remote(pairsend, pairbuf, pair_sem.at[0], pair_sem.at[1], partner)
    pair.start()

    got(half_slot(-2, 0), 0)
    copies[0].start()
    copies[1].start()
    got(half_slot(2, 1), 3)
    copies[2].start()
    copies[3].start()
    got(half_slot(-2, 1), 1)
    copies[4].start()
    got(half_slot(2, 0), 2)
    copies[5].start()
    share_chunk(slot(-2), -2).start()
    share_chunk(slot(2), 2).start()

    pair.wait_recv()
    share = share + pairbuf[...]
    h2send[...] = share
    h2buf[z] = share
    for k in range(1, nz):
        remote(h2send, h2buf.at[z], h2_ssem, h2_rsem, chip(k)).start()

    for k, n in ((-1, 4), (1, 5)):
        got(slot(k), n)
        share_chunk(slot(k), k).start()

    own_reflectors = exact(mixing_t, headbuf[...])
    bottom = exact(second_t, own_reflectors, TN)
    kernel_t = exact(second_t, mixing_t, TN)

    @pl.when(row != 0)
    def _():
        remote(obuf, obuf, o_ssem, o_rsem, {"row": 0}).wait_recv()

    own_base = exact(second_t, obuf[...])

    got(half_slot(4, 0), 10)
    got(half_slot(4, 1), 11)
    share_chunk(slot(4), 4).start()
    for k, n in ((-3, 6), (3, 8)):
        got(half_slot(k, 0), n)
        got(half_slot(k, 1), n + 1)
        share_chunk(slot(k), k).start()

    others(h2buf, nz, h2_ssem, h2_rsem).wait_recv()

    inner_total = h2buf[0]
    for c in range(1, nz):
        inner_total = inner_total + h2buf[c]
    inner_t = unpack(inner_total, lanes)[:, :nb]
    weight_t = -0.5 * exact(exact(second_t, inner_t), kernel_t)
    own_weights = own_base + exact(weight_t, headbuf[...])
    top_part = exact(mixing_t, own_weights, TN) + exact(weight_t, own_reflectors, TN)
    coefs[0:nb, :] = top_part
    coefs[nb : 2 * nb, :] = bottom
    coefs[2 * nb : 3 * nb, :] = wide(jnp.concatenate([weight_t, second_t], 1))
    coefs[3 * nb :, :] = jnp.where(row == 0, correction, 0.0)

    theirs = images.at[pl.ds((1 - core) * nz, nz)]
    remote(theirs, theirs, f_ssem, f_rsem, partner).wait_recv()

    keep.wait()

    remote(zout, pbuf, p_ssem, p_rsem.at[0], partner).wait_send()
    mine = images.at[pl.ds(0, nz)]
    remote(mine, mine, f_ssem, f_rsem, partner).wait_send()
    leaves(lambda copy: copy.wait_send())
    nears(lambda copy: copy.wait_send())
    for copy in stage_two:
        copy.wait_send()
    for copy in gather + copies:
        copy.wait_send()
    others(gbuf, nrow, g_ssem, g_rsem).wait_send()
    others(h1buf, nrow, h1_ssem, h1_rsem).wait_send()
    others(h2buf, nz, h2_ssem, h2_rsem).wait_send()
    pair.wait_send()

    @pl.when(row == 0)
    def _():
        heads = pv.at[:, pl.ds(0, 128 * (nrow - 1))]
        remote(heads, heads, t_ssem, t_rsem, partner).wait_send()
        remote(heads, heads, o_ssem, o_rsem, partner).wait_send()


def update_kernel(groups, slab, panel, images, coefs, updated, factor, uv, wv, out_sem):
    nb = 32
    parts = images.shape[0] // groups
    chunk = images.shape[2]
    length = parts * chunk

    def writes(g):
        span = pl.ds(g * length, length)
        return (
            pltpu.make_async_copy(wv.at[:, span], factor.at[:, span], out_sem.at[0, g]),
            pltpu.make_async_copy(uv.at[span, :], updated.at[span, :], out_sem.at[1, g]),
        )

    bh, bl = split(coefs[0 : 2 * nb, :])
    right = jnp.concatenate([bh, bl, bh], 0)
    ch, cl = split(coefs[2 * nb : 3 * nb, 0 : 2 * nb])
    left = jnp.concatenate([ch, ch, cl], 1)
    for g in range(groups):
        for i in range(g * parts, (g + 1) * parts):
            piece = slice(i * chunk, (i + 1) * chunk)
            columns = panel[:, piece]
            if i == 0:
                columns = jnp.concatenate(
                    [columns[:, 0:128] - coefs[3 * nb :, :], columns[:, 128:]], 1
                )
            xh, xl = split(jnp.concatenate([columns, images[i]], 0))
            wv[:, piece] = narrow(left, jnp.concatenate([xh, xl, xh], 0), NN)
            uv[piece, :] = slab[piece, :] - narrow(jnp.concatenate([xh, xh, xl], 0), right, TN)
        for copy in writes(g):
            copy.start()
    for g in range(groups):
        for copy in writes(g):
            copy.wait()


def local(nrow, ncol, slab, panel, far):
    nb, length = panel.shape
    chunk = length // ncol
    nz = ncol // 2
    anywhere = pl.BlockSpec(memory_space=pl.ANY)
    vmem = pl.BlockSpec(memory_space=pltpu.VMEM)
    dma = pltpu.SemaphoreType.DMA
    strip = pltpu.VMEM((nb, 128), F32)
    tile = pltpu.VMEM((8, 128), F32)

    def chunks(n, width=chunk):
        return pltpu.VMEM((n, nb, width), F32)

    images, coefs = pl.pallas_call(
        functools.partial(exchange_kernel, nrow, ncol),
        name="exchange",
        out_shape=(
            jax.ShapeDtypeStruct((ncol, nb, chunk), F32),
            jax.ShapeDtypeStruct((4 * nb, 128), F32),
        ),
        in_specs=[anywhere] * 3,
        out_specs=(anywhere, vmem),
        scratch_shapes=[
            pltpu.VMEM((nb, length), F32),
            pltpu.VMEM(slab.shape, F32),
            pltpu.VMEM((nb, chunk), F32),
            pltpu.VMEM((16, 128), F32),
            pltpu.VMEM((nrow, 16, 128), F32),
            strip,
            pltpu.VMEM((nb, length), F32),
            chunks(nz), chunks(nz), chunks(nz),
            chunks(2), chunks(2, chunk // 2), chunks(2), chunks(2), chunks(2),
            pltpu.VMEM((nb, chunk), F32),
            strip, strip,
            tile, pltpu.VMEM((nrow, 8, 128), F32),
            tile, pltpu.VMEM((nz, 8, 128), F32),
            tile, tile,
            dma((5,)),
            dma(()), dma(()),
            dma(()), dma(()),
            dma(()), dma((nz,)),
            dma((8,)), dma((8,)),
            dma((12,)), dma((12,)),
            dma(()), dma(()),
            dma(()), dma(()),
            dma(()), dma(()),
            dma(()), dma(()),
            dma((2,)), dma(()),
        ],
        compiler_params=pltpu.CompilerParams(
            collective_id=0, has_side_effects=True, vmem_limit_bytes=24 * 2**20
        ),
    )(*(pltpu.with_memory_space_constraint(array, pltpu.HBM) for array in (slab, panel, far)))
    groups = 4
    return pl.pallas_call(
        functools.partial(update_kernel, groups),
        name="update",
        out_shape=(
            jax.ShapeDtypeStruct(slab.shape, F32),
            jax.ShapeDtypeStruct(panel.shape, F32),
        ),
        in_specs=[vmem] * 4,
        out_specs=(anywhere, anywhere),
        scratch_shapes=[
            pltpu.VMEM(slab.shape, F32),
            pltpu.VMEM(panel.shape, F32),
            dma((2, groups)),
        ],
        compiler_params=pltpu.CompilerParams(vmem_limit_bytes=24 * 2**20),
    )(slab, panel, images, coefs)


def solution(mesh):
    sizes = dict(mesh.shape)
    body = functools.partial(local, sizes["row"], sizes["col"])
    in_specs = (P("row", "col"), P(None, "row"), P(None, "row"))
    out_specs = (P("row", "col"), P(None, "row"))
    return jax.shard_map(body, mesh=mesh, in_specs=in_specs, out_specs=out_specs, check_vma=False)
```

```python
import functools

import jax
import jax.numpy as jnp
from jax import lax
from jax.experimental import pallas as pl
from jax.experimental.pallas import tpu as pltpu
from jax.sharding import PartitionSpec as P

F32 = jnp.float32
BF16 = jnp.bfloat16
MESH = pl.DeviceIdType.MESH
NT = (((1,), (1,)), ((), ()))
TN = (((0,), (0,)), ((), ()))
NN = (((1,), (0,)), ((), ()))


def exact(left, right, dims=NN):
    return lax.dot_general(
        left, right, dims, precision=lax.Precision.HIGHEST, preferred_element_type=F32
    )


def narrow(left, right, dims):
    return lax.dot_general(left, right, dims, preferred_element_type=F32)


def split(x):
    high = x.astype(BF16)
    low = (x - high.astype(F32)).astype(BF16)
    return high, low


def split3(x):
    high = x.astype(BF16)
    rest = x - high.astype(F32)
    mid = rest.astype(BF16)
    low = (rest - mid.astype(F32)).astype(BF16)
    return high, mid, low


def gram_of(block):
    nb = block.shape[0]
    one, two, three = split3(block)
    first = narrow(jnp.concatenate([one, two, three], 0), one, NT)
    second = narrow(jnp.concatenate([one, two], 0), two, NT)
    third = narrow(one, three, NT)
    return (
        first[:nb]
        + (first[nb : 2 * nb] + second[:nb])
        + (first[2 * nb :] + second[nb:] + third)
    )


def cross(left, right):
    nb = left.shape[0]
    lh, ll = split(left)
    rh, rl = split(right)
    both = narrow(jnp.concatenate([lh, ll], 0), rh, NT)
    return both[:nb] + both[nb:] + narrow(lh, rl, NT)


def eliminate(tables, nb):
    rows = lax.broadcasted_iota(jnp.int32, (nb, 128), 0)
    for j in range(0, nb, 2):
        done = []
        for table in tables:
            column = jnp.broadcast_to(table[:, j : j + 1], (nb, 128))
            following = jnp.broadcast_to(table[:, j + 1 : j + 2], (nb, 128))
            pivot = column[j : j + 1, :]
            pivot_row = table[j : j + 1, :] / pivot
            below = jnp.where(rows > j, column, 0.0)
            following = following - below * (following[j : j + 1, :] / pivot)
            next_row = table[j + 1 : j + 2, :] - column[j + 1 : j + 2, :] * pivot_row
            next_row = next_row / following[j + 1 : j + 2, :]
            after = jnp.where(rows > j + 1, following, 0.0)
            done.append(table - below * pivot_row - after * next_row)
        tables = done
    return tables


def pack(square):
    total = square[0:8]
    for k in range(1, 4):
        total = total + pltpu.roll(square[8 * k : 8 * k + 8], 32 * k, 1)
    return total


def unpack(packed, lanes):
    parts = [packed] + [pltpu.roll(packed, 128 - 32 * k, 1) for k in range(1, 4)]
    return jnp.where(lanes < 32, jnp.concatenate(parts, 0), 0.0)


def wide(square):
    return jnp.concatenate([square, jnp.zeros((square.shape[0], 128 - square.shape[1]), F32)], 1)


def exchange_kernel(
    nrow, ncol,
    slab, panel, far,
    images, coefs,
    pv, sv, fv, gsend, gbuf, headbuf, pt, zout, pbuf, zsum,
    leaf3, leaf4, near, relay, twos, zown, osend, obuf, h1send, h1buf, h2send, h2buf, pairsend, pairbuf,
    load_sem, g_ssem, g_rsem, t_ssem, t_rsem, p_ssem, p_rsem, r_ssem, r_rsem,
    a_ssem, a_rsem, f_ssem, f_rsem, o_ssem, o_rsem, h1_ssem, h1_rsem, h2_ssem, h2_rsem,
    pair_sem, image_sem,
):
    nb = 32
    nz = ncol // 2
    chunk = pv.shape[1] // ncol
    half = chunk // 2
    row = lax.axis_index("row")
    col = lax.axis_index("col")
    z = lax.div(col, 2)
    core = lax.rem(col, 2)
    partner = {"col": col + 1 - 2 * core}
    rows = lax.broadcasted_iota(jnp.int32, (nb, 128), 0)
    lanes = lax.broadcasted_iota(jnp.int32, (nb, 128), 1)

    def remote(src, dst, ssem, rsem, device):
        return pltpu.make_async_remote_copy(
            src_ref=src, dst_ref=dst, send_sem=ssem, recv_sem=rsem,
            device_id=device, device_id_type=MESH,
        )

    def others(buffer, n, ssem, rsem):
        slots = buffer.at[pl.ds(0, n - 1)]
        return remote(slots, slots, ssem, rsem, partner)

    def row_peer(k):
        return lax.rem(row + k, nrow)

    def z_peer(k):
        return lax.rem(z + k + nz, nz)

    def chip(k):
        return {"col": 2 * z_peer(k) + core}

    load_p = pltpu.make_async_copy(panel, pv, load_sem.at[0])
    load_s = pltpu.make_async_copy(slab, sv, load_sem.at[1])
    own = core * nz + z
    own_columns = pl.ds(pl.multiple_of(own * chunk, chunk), chunk)
    load_f = pltpu.make_async_copy(far.at[:, own_columns], fv, load_sem.at[2])
    load_p.start()
    load_s.start()
    load_f.start()

    barrier = pltpu.get_barrier_semaphore()

    @pl.loop(1, nrow)
    def _(k):
        pl.semaphore_signal(barrier, inc=1, device_id={"row": row_peer(k)}, device_id_type=MESH)

    for device in (partner, chip(1), chip(-1), chip(2), chip(-2)):
        pl.semaphore_signal(barrier, inc=1, device_id=device, device_id_type=MESH)

    load_p.wait()
    gram = jnp.zeros((nb, nb), F32)
    for g in range(ncol):
        gram = gram + gram_of(pv[:, g * chunk : (g + 1) * chunk])
    gsend[0:8, :] = pack(wide(gram))
    gsend[8:16, :] = pack(jnp.where(lanes < nb, pv[:, 0:128], 0.0))
    gbuf[row] = gsend[...]
    pt[...] = pv[...]
    pl.semaphore_wait(barrier, nrow + 4)

    head_columns = pl.ds(pl.multiple_of(col * 128, 128), 128)

    @pl.when(row == 0)
    def _():
        for k in range(1, nrow):
            remote(pv.at[:, head_columns], headbuf, t_ssem, t_rsem, {"row": row_peer(k)}).start()

    for k in range(1, nrow):
        remote(gsend, gbuf.at[row], g_ssem, g_rsem, {"row": row_peer(k)}).start()

    @pl.when(row == 0)
    def _():
        local_head = pltpu.make_async_copy(pv.at[:, head_columns], headbuf, load_sem.at[3])
        local_head.start()
        local_head.wait()

    load_s.wait()

    @pl.when(row != 0)
    def _():
        remote(headbuf, headbuf, t_ssem, t_rsem, {"row": 0}).wait_recv()

    def produce():
        high, low = split(headbuf[...])
        weights = jnp.concatenate(
            [
                jnp.concatenate([high, high], 1),
                jnp.concatenate([low, jnp.zeros_like(low)], 1),
            ],
            0,
        )

        def product(index):
            block = sv[pl.ds(pl.multiple_of(index * chunk, chunk), chunk), :]
            sh, sl = split(block)
            both = narrow(weights, jnp.concatenate([sh, sl], 1), NT)
            return both[:nb] + both[nb:]

        def to_partner(peer):
            return remote(zout.at[peer], pbuf.at[peer], p_ssem, p_rsem.at[peer], partner)

        def other_half(k):
            peer = z_peer(k)
            zout[peer] = product((1 - core) * nz + peer)
            to_partner(peer).start()

        def own_half(k):
            peer = z_peer(k)
            part = product(core * nz + peer)
            to_partner(peer).wait_recv()
            zsum[peer] = part + pbuf[peer]

        pl.loop(3, nz)(other_half)
        pl.loop(3, nz - 2)(own_half)
        leaves(lambda copy: copy.start())
        pl.loop(nz, nz + 3)(other_half)
        pl.loop(nz - 2, nz + 3)(own_half)
        nears(lambda copy: copy.start())

    def leaves(act):
        act(remote(zsum.at[z_peer(-3)], leaf3.at[0], r_ssem.at[0], r_rsem.at[0], chip(-1)))
        act(remote(zsum.at[z_peer(3)], leaf3.at[1], r_ssem.at[1], r_rsem.at[1], chip(1)))
        first = zsum.at[z_peer(4), :, pl.ds(0, half)]
        second = zsum.at[z_peer(4), :, pl.ds(half, half)]
        act(remote(first, leaf4.at[0], r_ssem.at[2], r_rsem.at[2], chip(-2)))
        act(remote(second, leaf4.at[1], r_ssem.at[3], r_rsem.at[3], chip(2)))

    def nears(act):
        act(remote(zsum.at[z_peer(-1)], near.at[0], r_ssem.at[4], r_rsem.at[4], chip(-1)))
        act(remote(zsum.at[z_peer(1)], near.at[1], r_ssem.at[5], r_rsem.at[5], chip(1)))

    stage_two = (
        remote(relay.at[0], twos.at[0], r_ssem.at[6], r_rsem.at[6], chip(-2)),
        remote(relay.at[1], twos.at[1], r_ssem.at[7], r_rsem.at[7], chip(2)),
    )

    def arrived(index, slot):
        remote(slot, slot, r_ssem.at[index], r_rsem.at[index], partner).wait_recv()

    pl.when(z != 0)(produce)

    others(gbuf, nrow, g_ssem, g_rsem).wait_recv()

    total = gbuf[0, 0:8]
    for r in range(1, nrow):
        total = total + gbuf[r, 0:8]
    table = (
        unpack(total, lanes)
        + jnp.where(lanes == rows + nb, 1.0, 0.0)
        + pltpu.roll(unpack(gbuf[0, 8:16], lanes), 2 * nb, 1)
    )
    (table,) = eliminate([table], nb)
    pivots = jnp.sum(jnp.where(lanes == rows, table, 0.0), axis=1, keepdims=True)
    table = table / jnp.sqrt(pivots)
    signs = jnp.sum(jnp.where(lanes == rows + 2 * nb, table, 0.0), axis=1, keepdims=True)
    flip = jnp.where(signs >= 0.0, -1.0, 1.0).astype(F32)
    upper = jnp.where((lanes >= rows) & (lanes < nb), table * flip, 0.0)
    correction = wide(upper[:, :nb].T)

    @pl.when(col == 0)
    def _():
        headbuf[...] = headbuf[...] - correction

    pl.when(z == 0)(produce)

    @pl.when(row == 0)
    def _():
        pt[:, 0:128] = pt[:, 0:128] - correction

    arrived(0, leaf3.at[0])
    arrived(2, leaf4.at[0])
    low_side = zsum[z_peer(-2)] + leaf3[0]
    relay[0, :, 0:half] = low_side[:, 0:half] + leaf4[0]
    relay[0, :, half:] = low_side[:, half:]
    stage_two[0].start()
    arrived(1, leaf3.at[1])
    arrived(3, leaf4.at[1])
    high_side = zsum[z_peer(2)] + leaf3[1]
    relay[1, :, 0:half] = high_side[:, 0:half]
    relay[1, :, half:] = high_side[:, half:] + leaf4[1]
    stage_two[1].start()

    load_f.wait()
    inner = cross(fv[...], pt[:, own_columns])
    for g in range(nz):
        columns = pl.ds(pl.multiple_of((core * nz + g) * chunk, chunk), chunk)
        inner = inner + cross(zsum[g], pt[:, columns])
    h1send[...] = pack(wide(inner))
    h1buf[row] = h1send[...]

    for k in range(1, nrow):
        remote(h1send, h1buf.at[row], h1_ssem, h1_rsem, {"row": row_peer(k)}).start()

    @pl.when(row == 0)
    def _():
        extra = pltpu.make_async_copy(far.at[:, head_columns], obuf, load_sem.at[4])
        extra.start()
        head = sv.shape[1] * ncol
        ph, plow = split(pt[:, 0:head])
        sh, sl = split(sv[0:head, :])
        both = narrow(jnp.concatenate([ph, plow], 0), sh, NN)
        product = both[:nb] + both[nb:] + narrow(ph, sl, NN)
        extra.wait()
        osend[...] = product + obuf[...]
        obuf[...] = osend[...]

        for k in range(1, nrow):
            remote(osend, obuf, o_ssem, o_rsem, {"row": row_peer(k)}).start()

    flipped_inverse = (pltpu.roll(table, 128 - nb, 1) * flip)[:, :nb]
    shifted_t = jnp.where(lanes == rows, 1.0, 0.0) - jnp.where(
        lanes < nb, pltpu.roll(table, 128 - 2 * nb, 1) * flip, 0.0
    )
    shifted = wide(shifted_t[:, :nb].T)
    augment = jnp.where(lanes == rows + nb, 1.0, 0.0)
    lower_table, upper_table = eliminate([shifted + augment, shifted_t + augment], nb)
    diagonal = jnp.sum(jnp.where(lanes == rows, upper_table, 0.0), axis=1, keepdims=True)
    lower_inverse = pltpu.roll(lower_table, 128 - nb, 1)[:, :nb]
    upper_inverse_t = (pltpu.roll(upper_table, 128 - nb, 1) / diagonal)[:, :nb]
    mixing_t = -exact(upper_inverse_t, flipped_inverse)
    second_t = -exact(lower_inverse, flipped_inverse)

    arrived(4, near.at[0])
    arrived(5, near.at[1])
    arrived(6, twos.at[0])
    arrived(7, twos.at[1])
    zown[...] = (fv[...] + zsum[z]) + (near[0] + near[1]) + (twos[0] + twos[1])

    def slot(k):
        return images.at[core * nz + z_peer(k)]

    def half_slot(k, part):
        return images.at[core * nz + z_peer(k), :, pl.ds(part * half, half)]

    def half_own(part):
        return zown.at[:, pl.ds(part * half, half)]

    def got(ref, n):
        remote(ref, ref, a_ssem.at[0], a_rsem.at[n], partner).wait_recv()

    def onward(k, part, n, m, device):
        piece = half_slot(k, part)
        return remote(piece, piece, a_ssem.at[n], a_rsem.at[m], device)

    gather = (
        remote(half_own(0), half_slot(0, 0), a_ssem.at[0], a_rsem.at[0], chip(2)),
        remote(half_own(1), half_slot(0, 1), a_ssem.at[1], a_rsem.at[3], chip(-2)),
        remote(half_own(1), half_slot(0, 1), a_ssem.at[2], a_rsem.at[1], chip(2)),
        remote(half_own(0), half_slot(0, 0), a_ssem.at[3], a_rsem.at[2], chip(-2)),
        remote(zown, slot(0), a_ssem.at[4], a_rsem.at[4], chip(1)),
        remote(zown, slot(0), a_ssem.at[5], a_rsem.at[5], chip(-1)),
    )
    copies = (
        onward(-2, 0, 6, 10, chip(2)),
        onward(-2, 0, 7, 6, chip(1)),
        onward(2, 1, 8, 11, chip(-2)),
        onward(2, 1, 9, 9, chip(-1)),
        onward(-2, 1, 10, 7, chip(1)),
        onward(2, 0, 11, 8, chip(-1)),
    )

    def share_chunk(src, k):
        return remote(src, slot(k), f_ssem, f_rsem, partner)

    for copy in gather:
        copy.start()
    keep = pltpu.make_async_copy(zown, slot(0), image_sem)
    keep.start()
    share_chunk(zown, 0).start()
    others(h1buf, nrow, h1_ssem, h1_rsem).wait_recv()
    share = h1buf[0]
    for r in range(1, nrow):
        share = share + h1buf[r]
    pairsend[...] = share
    pair = remote(pairsend, pairbuf, pair_sem.at[0], pair_sem.at[1], partner)
    pair.start()

    got(half_slot(-2, 0), 0)
    copies[0].start()
    copies[1].start()
    got(half_slot(2, 1), 3)
    copies[2].start()
    copies[3].start()
    got(half_slot(-2, 1), 1)
    copies[4].start()
    got(half_slot(2, 0), 2)
    copies[5].start()
    share_chunk(slot(-2), -2).start()
    share_chunk(slot(2), 2).start()

    pair.wait_recv()
    share = share + pairbuf[...]
    h2send[...] = share
    h2buf[z] = share
    for k in range(1, nz):
        remote(h2send, h2buf.at[z], h2_ssem, h2_rsem, chip(k)).start()

    for k, n in ((-1, 4), (1, 5)):
        got(slot(k), n)
        share_chunk(slot(k), k).start()

    own_reflectors = exact(mixing_t, headbuf[...])
    bottom = exact(second_t, own_reflectors, TN)
    kernel_t = exact(second_t, mixing_t, TN)

    @pl.when(row != 0)
    def _():
        remote(obuf, obuf, o_ssem, o_rsem, {"row": 0}).wait_recv()

    own_base = exact(second_t, obuf[...])

    for k, n in ((-3, 6), (3, 8)):
        got(half_slot(k, 0), n)
        got(half_slot(k, 1), n + 1)
        share_chunk(slot(k), k).start()
    got(half_slot(4, 0), 10)
    got(half_slot(4, 1), 11)
    share_chunk(slot(4), 4).start()

    others(h2buf, nz, h2_ssem, h2_rsem).wait_recv()

    inner_total = h2buf[0]
    for c in range(1, nz):
        inner_total = inner_total + h2buf[c]
    inner_t = unpack(inner_total, lanes)[:, :nb]
    weight_t = -0.5 * exact(exact(second_t, inner_t), kernel_t)
    own_weights = own_base + exact(weight_t, headbuf[...])
    top_part = exact(mixing_t, own_weights, TN) + exact(weight_t, own_reflectors, TN)
    coefs[0:nb, :] = top_part
    coefs[nb : 2 * nb, :] = bottom
    coefs[2 * nb : 3 * nb, :] = wide(jnp.concatenate([weight_t, second_t], 1))
    coefs[3 * nb :, :] = jnp.where(row == 0, correction, 0.0)

    theirs = images.at[pl.ds((1 - core) * nz, nz)]
    remote(theirs, theirs, f_ssem, f_rsem, partner).wait_recv()

    keep.wait()

    remote(zout, pbuf, p_ssem, p_rsem.at[0], partner).wait_send()
    mine = images.at[pl.ds(0, nz)]
    remote(mine, mine, f_ssem, f_rsem, partner).wait_send()
    leaves(lambda copy: copy.wait_send())
    nears(lambda copy: copy.wait_send())
    for copy in stage_two:
        copy.wait_send()
    for copy in gather + copies:
        copy.wait_send()
    others(gbuf, nrow, g_ssem, g_rsem).wait_send()
    others(h1buf, nrow, h1_ssem, h1_rsem).wait_send()
    others(h2buf, nz, h2_ssem, h2_rsem).wait_send()
    pair.wait_send()

    @pl.when(row == 0)
    def _():
        heads = pv.at[:, pl.ds(0, 128 * (nrow - 1))]
        remote(heads, heads, t_ssem, t_rsem, partner).wait_send()
        remote(heads, heads, o_ssem, o_rsem, partner).wait_send()


def update_kernel(groups, slab, panel, images, coefs, updated, factor, uv, wv, out_sem):
    nb = 32
    parts = images.shape[0] // groups
    chunk = images.shape[2]
    length = parts * chunk

    def writes(g):
        span = pl.ds(g * length, length)
        return (
            pltpu.make_async_copy(wv.at[:, span], factor.at[:, span], out_sem.at[0, g]),
            pltpu.make_async_copy(uv.at[span, :], updated.at[span, :], out_sem.at[1, g]),
        )

    bh, bl = split(coefs[0 : 2 * nb, :])
    right = jnp.concatenate([bh, bl, bh], 0)
    ch, cl = split(coefs[2 * nb : 3 * nb, 0 : 2 * nb])
    left = jnp.concatenate([ch, ch, cl], 1)
    for g in range(groups):
        for i in range(g * parts, (g + 1) * parts):
            piece = slice(i * chunk, (i + 1) * chunk)
            columns = panel[:, piece]
            if i == 0:
                columns = jnp.concatenate(
                    [columns[:, 0:128] - coefs[3 * nb :, :], columns[:, 128:]], 1
                )
            xh, xl = split(jnp.concatenate([columns, images[i]], 0))
            wv[:, piece] = narrow(left, jnp.concatenate([xh, xl, xh], 0), NN)
            uv[piece, :] = slab[piece, :] - narrow(jnp.concatenate([xh, xh, xl], 0), right, TN)
        for copy in writes(g):
            copy.start()
    for g in range(groups):
        for copy in writes(g):
            copy.wait()


def local(nrow, ncol, slab, panel, far):
    nb, length = panel.shape
    chunk = length // ncol
    nz = ncol // 2
    anywhere = pl.BlockSpec(memory_space=pl.ANY)
    vmem = pl.BlockSpec(memory_space=pltpu.VMEM)
    dma = pltpu.SemaphoreType.DMA
    strip = pltpu.VMEM((nb, 128), F32)
    tile = pltpu.VMEM((8, 128), F32)

    def chunks(n, width=chunk):
        return pltpu.VMEM((n, nb, width), F32)

    images, coefs = pl.pallas_call(
        functools.partial(exchange_kernel, nrow, ncol),
        name="exchange",
        out_shape=(
            jax.ShapeDtypeStruct((ncol, nb, chunk), F32),
            jax.ShapeDtypeStruct((4 * nb, 128), F32),
        ),
        in_specs=[anywhere] * 3,
        out_specs=(anywhere, vmem),
        scratch_shapes=[
            pltpu.VMEM((nb, length), F32),
            pltpu.VMEM(slab.shape, F32),
            pltpu.VMEM((nb, chunk), F32),
            pltpu.VMEM((16, 128), F32),
            pltpu.VMEM((nrow, 16, 128), F32),
            strip,
            pltpu.VMEM((nb, length), F32),
            chunks(nz), chunks(nz), chunks(nz),
            chunks(2), chunks(2, chunk // 2), chunks(2), chunks(2), chunks(2),
            pltpu.VMEM((nb, chunk), F32),
            strip, strip,
            tile, pltpu.VMEM((nrow, 8, 128), F32),
            tile, pltpu.VMEM((nz, 8, 128), F32),
            tile, tile,
            dma((5,)),
            dma(()), dma(()),
            dma(()), dma(()),
            dma(()), dma((nz,)),
            dma((8,)), dma((8,)),
            dma((12,)), dma((12,)),
            dma(()), dma(()),
            dma(()), dma(()),
            dma(()), dma(()),
            dma(()), dma(()),
            dma((2,)), dma(()),
        ],
        compiler_params=pltpu.CompilerParams(
            collective_id=0, has_side_effects=True, vmem_limit_bytes=24 * 2**20
        ),
    )(*(pltpu.with_memory_space_constraint(array, pltpu.HBM) for array in (slab, panel, far)))
    groups = 4
    return pl.pallas_call(
        functools.partial(update_kernel, groups),
        name="update",
        out_shape=(
            jax.ShapeDtypeStruct(slab.shape, F32),
            jax.ShapeDtypeStruct(panel.shape, F32),
        ),
        in_specs=[vmem] * 4,
        out_specs=(anywhere, anywhere),
        scratch_shapes=[
            pltpu.VMEM(slab.shape, F32),
            pltpu.VMEM(panel.shape, F32),
            dma((2, groups)),
        ],
        compiler_params=pltpu.CompilerParams(vmem_limit_bytes=24 * 2**20),
    )(slab, panel, images, coefs)


def solution(mesh):
    sizes = dict(mesh.shape)
    body = functools.partial(local, sizes["row"], sizes["col"])
    in_specs = (P("row", "col"), P(None, "row"), P(None, "row"))
    out_specs = (P("row", "col"), P(None, "row"))
    return jax.shard_map(body, mesh=mesh, in_specs=in_specs, out_specs=out_specs, check_vma=False)
```
